128 devices in a mesh: row: 16 (over z, y), col: 8 (over x, core).
Axes of the slice: x: 4, y: 4, z: 4, core: 2. Of those that a mesh axis runs over, the one named last changes fastest.
Arguments:
- trail_adjoint: float32 [16384, 16384], P('row', 'col'), may hold values from -6 to 6
- lower_new: float32 [16384, 256], P('row', 'col'), may hold values from -0.046875 to 0.046875
- upper_new: float32 [256, 16384], P('row', 'col'), may hold values from -0.046875 to 0.046875
- lower_old_top: float32 [256, 256], replicated, may hold values from -0.375 to 0.375
- lower_old: float32 [16384, 256], P('row', 'col'), may hold values from -0.046875 to 0.046875
- upper_old_left: float32 [256, 256], replicated, may hold values from -0.375 to 0.375
- upper_old: float32 [256, 16384], P('row', 'col'), may hold values from -0.046875 to 0.046875
- diag_lower_new: float32 [256, 256], replicated, as said below
- diag_upper_new: float32 [256, 256], replicated, as said below
- inverse_lower_new: float32 [256, 256], replicated, as said below
- inverse_upper_new: float32 [256, 256], replicated, as said below
- diag_lower_old: float32 [256, 256], replicated, as said below
- diag_upper_old: float32 [256, 256], replicated, as said below
- inverse_lower_old: float32 [256, 256], replicated, as said below
- inverse_upper_old: float32 [256, 256], replicated, as said below
Outputs:
- corner_old: float32 [256, 256], replicated
- strip_top: float32 [256, 256], replicated
- strip_bottom: float32 [16384, 256], P(('row', 'col'))
- band_left: float32 [256, 256], replicated
- band_right: float32 [256, 16384], P(None, 'col')
The draws below stay inside these ranges and needn't reach their ends.
Inputs may be any that keep to these rules, and one draw needn't show every extreme that they name: `diag_lower_new`: unit lower triangular. `diag_upper_new`: upper triangular, diagonal from 1 to 2. `inverse_lower_new`: the inverse of diag_lower_new. `inverse_upper_new`: the inverse of diag_upper_new. `diag_lower_old`: unit lower triangular. `diag_upper_old`: upper triangular, diagonal from 1 to 2. `inverse_lower_old`: the inverse of diag_lower_old. `inverse_upper_old`: the inverse of diag_upper_old.
All inputs are finite; a program needn't handle non-finite values.
Results may differ from the reference program's by a relative error of at most 0.000075.
Values sent between devices are 32-bit elements; how exact they have to be, the bound alone decides.
No kernel may reach another device: no remote copies, remote signals or barrier semaphores. Data moves between devices by JAX's collectives and lax.ppermute only.
A program may use at most 128 MiB of HBM per device.

```python
import math
import jax
import jax.numpy as jnp
from jax import lax

B = 256
M = 16384


def triangle_pair(key, marker, downward):
    folded = jax.random.fold_in(key, marker)
    seed_noise, seed_scale = jax.random.split(folded)
    noise = jax.random.normal(seed_noise, (B, B), jnp.float32) * (0.3 / math.sqrt(B))
    identity = jnp.eye(B, dtype=jnp.float32)
    if downward:
        factor = jnp.tril(noise, -1) + identity
    else:
        scales = jax.random.uniform(seed_scale, (B,), jnp.float32, 1.0, 2.0)
        factor = jnp.triu(noise, 1) + jnp.diag(scales)
    inverse = jax.scipy.linalg.solve_triangular(factor, identity, lower=downward)
    return (factor, inverse)


def draw_diag_lower_new(key, part):
    return triangle_pair(key, 1, True)[0]


def draw_inverse_lower_new(key, part):
    return triangle_pair(key, 1, True)[1]


def draw_diag_upper_new(key, part):
    return triangle_pair(key, 2, False)[0]


def draw_inverse_upper_new(key, part):
    return triangle_pair(key, 2, False)[1]


def draw_diag_lower_old(key, part):
    return triangle_pair(key, 3, True)[0]


def draw_inverse_lower_old(key, part):
    return triangle_pair(key, 3, True)[1]


def draw_diag_upper_old(key, part):
    return triangle_pair(key, 4, False)[0]


def draw_inverse_upper_old(key, part):
    return triangle_pair(key, 4, False)[1]


def raised(entries, rng, source, target, parts, factor):
    def block_of(axis_at):
        return (jnp.arange(entries.shape[axis_at]) // (entries.shape[axis_at] // parts)).reshape((-1,) + (1,) * (entries.ndim - 1 - axis_at))

    first = jax.random.permutation(rng, parts)[block_of(target)]
    second = (block_of(target) + parts // 2) % parts
    return jnp.where((block_of(source) == first) | (block_of(source) == second), factor * entries, entries)


def block_levels(stream_key, dims, pieces, low, largest):
    gain = 1.0
    for dim, shards_of in pieces:
        heights = jax.random.uniform(jax.random.fold_in(jax.random.fold_in(stream_key, 6), dim), (shards_of,), jnp.float32, low / len(pieces), largest / len(pieces))
        gain = gain * jnp.repeat(jnp.exp(heights), dims[dim] // shards_of).reshape((-1,) + (1,) * (len(dims) - 1 - dim))
    return gain


def gaussian(own_key, shape, scale, bound, pieces=(), held_as=jnp.bfloat16):
    drawn = scale * jax.random.normal(own_key, shape, jnp.float32)
    if pieces:
        drawn = drawn * block_levels(own_key, shape, pieces, -0.22, 0.18)
    return jnp.clip(drawn, -bound, bound).astype(held_as)


def noise_with(own_key, extent, spread, bound, shards, heavy, kind=jnp.bfloat16):
    drawn = spread * jax.random.normal(own_key, extent, jnp.float32)
    if shards:
        drawn = drawn * block_levels(own_key, extent, shards, -0.22, 0.18)
    return jnp.clip(raised(drawn, jax.random.fold_in(own_key, 3), *heavy), -bound, bound).astype(kind)


def setup_inputs(seed: int = 0) -> dict:
    streams_of = jax.random.split(jax.random.key(seed), 16)
    trail_adjoint = noise_with(streams_of[0], (M, M), 1.0, 6.0, ((0, 16), (1, 8)), (1, 0, 16, 2.0), jnp.float32)
    lower_new = gaussian(streams_of[1], (M, B), M ** -0.5, 0.046875, ((0, 16), (1, 8)), jnp.float32)
    upper_new = gaussian(streams_of[2], (B, M), M ** -0.5, 0.046875, ((0, 16), (1, 8)), jnp.float32)
    lower_old_top = gaussian(streams_of[3], (B, B), B ** -0.5, 0.375, (), jnp.float32)
    lower_old = gaussian(streams_of[4], (M, B), M ** -0.5, 0.046875, ((0, 16), (1, 8)), jnp.float32)
    upper_old_left = gaussian(streams_of[5], (B, B), B ** -0.5, 0.375, (), jnp.float32)
    upper_old = gaussian(streams_of[6], (B, M), M ** -0.5, 0.046875, ((0, 16), (1, 8)), jnp.float32)
    diag_lower_new = draw_diag_lower_new(jax.random.fold_in(streams_of[15], 71), 0)
    diag_upper_new = draw_diag_upper_new(jax.random.fold_in(streams_of[15], 71), 0)
    inverse_lower_new = draw_inverse_lower_new(jax.random.fold_in(streams_of[15], 71), 0)
    inverse_upper_new = draw_inverse_upper_new(jax.random.fold_in(streams_of[15], 71), 0)
    diag_lower_old = draw_diag_lower_old(jax.random.fold_in(streams_of[15], 71), 0)
    diag_upper_old = draw_diag_upper_old(jax.random.fold_in(streams_of[15], 71), 0)
    inverse_lower_old = draw_inverse_lower_old(jax.random.fold_in(streams_of[15], 71), 0)
    inverse_upper_old = draw_inverse_upper_old(jax.random.fold_in(streams_of[15], 71), 0)
    return dict(trail_adjoint=trail_adjoint, lower_new=lower_new, upper_new=upper_new, lower_old_top=lower_old_top, lower_old=lower_old, upper_old_left=upper_old_left, upper_old=upper_old, diag_lower_new=diag_lower_new, diag_upper_new=diag_upper_new, inverse_lower_new=inverse_lower_new, inverse_upper_new=inverse_upper_new, diag_lower_old=diag_lower_old, diag_upper_old=diag_upper_old, inverse_lower_old=inverse_lower_old, inverse_upper_old=inverse_upper_old)


precise = lax.Precision.HIGHEST

def product(left, right):
    return jnp.dot(left, right, precision=precise)

def diag_adjoint(lower_factor, upper_factor, lower_inverse, upper_inverse, lower_grad, upper_grad):
    inner = jnp.tril(product(lower_factor.T, lower_grad), -1) + jnp.triu(product(upper_grad, upper_factor.T))
    return product(product(lower_inverse.T, inner), upper_inverse.T)

def reference(trail_adjoint, lower_new, upper_new, lower_old_top, lower_old, upper_old_left, upper_old, diag_lower_new, diag_upper_new, inverse_lower_new, inverse_upper_new, diag_lower_old, diag_upper_old, inverse_lower_old, inverse_upper_old):
    lower_adj_new = -product(trail_adjoint, upper_new.T)
    upper_adj_new = -product(lower_new.T, trail_adjoint)
    strip_new = product(lower_adj_new, inverse_upper_new.T)
    band_new = product(inverse_lower_new.T, upper_adj_new)
    corner_new = diag_adjoint(diag_lower_new, diag_upper_new, inverse_lower_new, inverse_upper_new, -product(band_new, upper_new.T), -product(lower_new.T, strip_new))
    strip_top = product(-(product(corner_new, upper_old_left.T) + product(band_new, upper_old.T)), inverse_upper_old.T)
    strip_bottom = product(-(product(strip_new, upper_old_left.T) + product(trail_adjoint, upper_old.T)), inverse_upper_old.T)
    band_left = product(inverse_lower_old.T, -(product(lower_old_top.T, corner_new) + product(lower_old.T, strip_new)))
    band_right = product(inverse_lower_old.T, -(product(lower_old_top.T, band_new) + product(lower_old.T, trail_adjoint)))
    lower_grad = -(product(band_left, upper_old_left.T) + product(band_right, upper_old.T))
    upper_grad = -(product(lower_old_top.T, strip_top) + product(lower_old.T, strip_bottom))
    corner_old = diag_adjoint(diag_lower_old, diag_upper_old, inverse_lower_old, inverse_upper_old, lower_grad, upper_grad)
    return (corner_old, strip_top, strip_bottom, band_left, band_right)
```

```python
import jax
import jax.numpy as jnp
from jax import lax
from jax.sharding import Mesh, PartitionSpec as P

exact = lax.Precision.HIGHEST
close = lax.Precision.HIGH


def dot(left, right, dims, precision=exact):
    return lax.dot_general(
        left, right, (dims, ((), ())), precision=precision, preferred_element_type=jnp.float32
    )


def nn(left, right, precision=exact):
    return dot(left, right, ((1,), (0,)), precision)


def nt(left, right, precision=exact):
    return dot(left, right, ((1,), (1,)), precision)


def tn(left, right, precision=exact):
    return dot(left, right, ((0,), (0,)), precision)


def swap(value, axis, step):
    size = lax.axis_size(axis)
    return lax.ppermute(value, axis, [(i, i ^ step) for i in range(size)])


def block(value, index, size):
    return lax.dynamic_slice_in_dim(value, index * size, size, 0)


def scatter_sum(value, axis):
    parts = lax.axis_size(axis)
    me = lax.axis_index(axis)
    size = value.shape[0] // parts
    total = block(value, me, size)
    for step in range(1, parts):
        total = total + swap(block(value, me ^ step, size), axis, step)
    return total


def gather(value, axis):
    parts = lax.axis_size(axis)
    me = lax.axis_index(axis)
    size = value.shape[0]
    out = jnp.zeros((parts * size, *value.shape[1:]), value.dtype)
    out = lax.dynamic_update_slice_in_dim(out, value, me * size, 0)
    for step in range(1, parts):
        out = lax.dynamic_update_slice_in_dim(out, swap(value, axis, step), (me ^ step) * size, 0)
    return out


def gather_inner(value, axis):
    parts = lax.axis_size(axis)
    me = lax.axis_index(axis)
    value = value[:, None]
    out = jnp.zeros((value.shape[0], parts, *value.shape[2:]), value.dtype)
    out = lax.dynamic_update_slice_in_dim(out, value, me, 1)
    for step in range(1, parts):
        out = lax.dynamic_update_slice_in_dim(out, swap(value, axis, step), me ^ step, 1)
    return out


def total(value, axis):
    first = swap(value, axis, 1)
    second = swap(value, axis, 2)
    third = swap(value, axis, 3)
    return (value + first) + (second + third)


def body(
    trail,
    lower_new,
    upper_new,
    lot,
    lower_old,
    uol,
    upper_old,
    ldn,
    udn,
    lin,
    uin,
    ldo,
    udo,
    lio,
    uio,
):
    width = lin.shape[0]
    rows, columns = trail.shape

    near = gather(upper_new, "z").reshape(4, -1, columns)
    upper_full_new = gather_inner(near, "y").reshape(width, columns)
    upper_full_old = gather(gather(upper_old, "y"), "z")
    upper_stack = jnp.concatenate((upper_full_new, upper_full_old), axis=0)

    lower_mine = jnp.concatenate((lower_new.T, lower_old.T), axis=0)
    lower_stack = lax.all_gather(lower_mine, ("x", "c"), axis=0, tiled=True)
    lower_stack = lower_stack.reshape(8, 2, -1, rows).transpose(1, 0, 2, 3).reshape(2 * width, rows)

    upper_pair = tn(uol, uio.T)
    upper_triple = tn(uin, upper_pair)
    lower_pair = tn(lio, lot.T)
    lower_triple = nt(lower_pair, lin)
    lower_unit = tn(ldn, lin.T)
    upper_unit = tn(uin, udn.T)

    weights = jnp.concatenate((lower_triple, -lio.T), axis=1)
    band = nn(nn(weights, lower_stack, close), trail, close)
    half = width // 2
    first = scatter_sum(scatter_sum(band[:half], "z"), "y")
    second = scatter_sum(scatter_sum(band[half:], "y"), "z")
    band_right = jnp.concatenate(
        (gather(gather(first, "y"), "z"), gather(gather(second, "z"), "y")), axis=0
    )

    right = nt(trail, upper_stack, close)
    inner = nn(lower_stack, right, close)
    strip = nn(right, jnp.concatenate((upper_triple, -uio.T), axis=0), close)
    strip_bottom = lax.psum_scatter(strip, ("x", "c"), scatter_dimension=0, tiled=True)

    inner = scatter_sum(scatter_sum(inner, "c"), "x")
    inner = total(total(inner, "y"), "z")
    inner = gather(gather(inner, "x"), "c")
    g11, g12 = inner[:width, :width], inner[:width, width:]
    g21, g22 = inner[width:, :width], inner[width:, width:]

    corner_new = nt(tn(lin, jnp.tril(nn(lower_unit, g11), -1) + jnp.triu(nn(g11, upper_unit))), uin)
    strip_top = nt(tn(lin, g12), uio) - nn(corner_new, upper_pair)
    band_left = tn(lio, nt(g21, uin)) - nn(lower_pair, corner_new)
    outer_old = nn(lower_triple, g12) - tn(lio, g22)
    inner_old = nn(g21, upper_triple) - nt(g22, uio)
    lower_grad = -(nt(band_left, uol) + outer_old)
    upper_grad = -(tn(lot, strip_top) + inner_old)
    inside = jnp.tril(tn(ldo, lower_grad), -1) + jnp.triu(nt(upper_grad, udo))
    corner_old = nt(tn(lio, inside), uio)
    return corner_old, strip_top, strip_bottom, band_left, band_right


def solution(mesh):
    fine = Mesh(mesh.devices.reshape(4, 4, 4, 2), ("z", "y", "x", "c"))
    row, col = ("z", "y"), ("x", "c")
    split, whole = P(row, col), P()
    return jax.shard_map(
        body,
        mesh=fine,
        in_specs=(split, split, split, whole, split, whole, split) + (whole,) * 8,
        out_specs=(whole, whole, P(row + col, None), whole, P(None, col)),
        check_vma=False,
    )
```

```python
import functools

import jax
import jax.numpy as jnp
from jax import lax
from jax.experimental import pallas as pl
from jax.experimental.pallas import tpu as pltpu
from jax.sharding import Mesh, PartitionSpec as P

HALF = jnp.bfloat16
FULL = jnp.float32
VMEM = pl.BlockSpec(memory_space=pltpu.VMEM)


def mul(left, right, dims):
    return lax.dot_general(left, right, (dims, ((), ())), preferred_element_type=FULL)


def exact(left, right, dims=((1,), (0,))):
    return lax.dot_general(
        left,
        right,
        (dims, ((), ())),
        precision=lax.Precision.HIGHEST,
        preferred_element_type=FULL,
    )


def parts(value):
    high = value.astype(HALF)
    return high, (value - high.astype(FULL)).astype(HALF)


def close(left, right, dims=((1,), (0,))):
    (lh, ll), (rh, rl) = left, right
    return mul(lh, rl, dims) + mul(ll, rh, dims) + mul(lh, rh, dims)


X_NEW, Y_NEW, U_PAIR, U_TRIPLE, L_PAIR, L_TRIPLE = range(6)


def prepare_kernel(lot, uol, ldn, udn, lin, uin, lio, uio, out):
    upper_pair = exact(uol[...].T, uio[...].T)
    lower_pair = exact(lio[...].T, lot[...].T)
    out[X_NEW] = exact(ldn[...].T, lin[...].T)
    out[Y_NEW] = exact(uin[...].T, udn[...].T)
    out[U_PAIR] = upper_pair
    out[L_PAIR] = lower_pair
    out[U_TRIPLE] = exact(uin[...].T, upper_pair)
    out[L_TRIPLE] = exact(lower_pair, lin[...].T)


def prepare(*factors):
    width = factors[0].shape[0]
    return pl.pallas_call(
        prepare_kernel,
        out_shape=jax.ShapeDtypeStruct((6, width, width), FULL),
        in_specs=[VMEM] * len(factors),
        out_specs=VMEM,
        name="prepare",
        cost_estimate=pl.CostEstimate(
            flops=72 * width**3, bytes_accessed=56 * width**2, transcendentals=0
        ),
    )(*factors)


def lower_rows(lower, panel, count, piece):
    return jnp.concatenate(
        [
            lower[pl.ds((2 * k + panel) * piece, piece), :]
            for k in range(count)
        ],
        axis=0,
    )


def band_kernel(count, small, lio, lower, trail, out, weight_high, weight_low):
    width = lio.shape[0]
    piece = width // count

    @pl.when(pl.program_id(0) == 0)
    def _():
        new = parts(lower_rows(lower, 0, count, piece))
        old = parts(lower_rows(lower, 1, count, piece))
        weight = close(parts(small[0]), new) - close(parts(lio[...].T), old)
        high, low = parts(weight)
        weight_high[...] = high
        weight_low[...] = low

    band = close((weight_high[...], weight_low[...]), parts(trail[...]))
    size = out.shape[1] // 2
    for k in range(16):
        turned = 4 * (k % 4) + k // 4
        first, second = k * size, width // 2 + turned * size
        out[k, :size, :] = band[first : first + size, :]
        out[k, size:, :] = band[second : second + size, :]


def band_products(small, lio, lower, trail, ranks, count, tile=512):
    rows, columns = trail.shape
    width = lio.shape[0]
    return pl.pallas_call(
        functools.partial(band_kernel, count),
        out_shape=jax.ShapeDtypeStruct((ranks, width // ranks, columns), FULL),
        grid=(columns // tile,),
        in_specs=[
            pl.BlockSpec((1, width, width), lambda j: (L_TRIPLE, 0, 0)),
            pl.BlockSpec((width, width), lambda j: (0, 0)),
            pl.BlockSpec((2 * width, rows), lambda j: (0, 0)),
            pl.BlockSpec((rows, tile), lambda j: (0, j)),
        ],
        out_specs=pl.BlockSpec((ranks, width // ranks, tile), lambda j: (0, 0, j)),
        scratch_shapes=[pltpu.VMEM((width, rows), HALF)] * 2,
        compiler_params=pltpu.CompilerParams(vmem_limit_bytes=48 << 20),
        name="band_products",
        cost_estimate=pl.CostEstimate(
            flops=6 * width * rows * columns,
            bytes_accessed=4 * (rows * columns + 2 * width * rows + width * columns),
            transcendentals=0,
        ),
    )(small, lio, lower, trail)


def panel_kernel(count, place, small, uio, lower, trail, *rest):
    pieces, (inner, strip, upper_high, upper_low, side_high, side_low) = rest[:8], rest[8:]
    width = uio.shape[0]
    z, y = place[0], place[1]

    @pl.when(pl.program_id(0) == 0)
    def _():
        inner[...] = jnp.zeros_like(inner)
        high, low = parts(small[0])
        side_high[:width, :] = high
        side_low[:width, :] = low
        high, low = parts(-uio[...].T)
        side_high[width:, :] = high
        side_low[width:, :] = low
        for k in range(4):
            high, low = parts(pieces[k][...])
            chunk = high.shape[0] // 4
            for zz in range(4):
                at = pl.ds(pl.multiple_of((4 * zz + (y ^ k)) * chunk, chunk), chunk)
                upper_high[at, :] = high[zz * chunk : (zz + 1) * chunk, :]
                upper_low[at, :] = low[zz * chunk : (zz + 1) * chunk, :]
            high, low = parts(pieces[4 + k][...])
            size = high.shape[0]
            at = pl.ds(pl.multiple_of(width + (z ^ k) * size, size), size)
            upper_high[at, :] = high
            upper_low[at, :] = low

    product = close(parts(trail[...]), (upper_high[...], upper_low[...]), ((1,), (1,)))
    product = parts(product)
    strip[...] = close(product, (side_high[...], side_low[...]))
    piece = width // count
    for panel in range(2):
        left = parts(lower_rows(lower, panel, count, piece))
        inner[panel * width : (panel + 1) * width, :] += close(left, product)


def panel_products(place, small, uio, lower, trail, pieces, count, tile=256):
    rows, columns = trail.shape
    width = uio.shape[0]
    once = pl.Buffered(1)
    size = pieces[0].shape[0]
    return pl.pallas_call(
        functools.partial(panel_kernel, count),
        out_shape=(
            jax.ShapeDtypeStruct((2 * width, 2 * width), FULL),
            jax.ShapeDtypeStruct((rows, width), FULL),
        ),
        grid_spec=pltpu.PrefetchScalarGridSpec(
            num_scalar_prefetch=1,
            grid=(rows // tile,),
            in_specs=[
                pl.BlockSpec((1, width, width), lambda i, p: (U_TRIPLE, 0, 0)),
                pl.BlockSpec((width, width), lambda i, p: (0, 0)),
                pl.BlockSpec((2 * width, tile), lambda i, p: (0, i)),
                pl.BlockSpec((tile, columns), lambda i, p: (i, 0)),
            ]
            + [pl.BlockSpec((size, columns), lambda i, p: (0, 0), pipeline_mode=once)] * 8,
            out_specs=(
                pl.BlockSpec((2 * width, 2 * width), lambda i, p: (0, 0)),
                pl.BlockSpec((tile, width), lambda i, p: (i, 0)),
            ),
            scratch_shapes=[pltpu.VMEM((2 * width, columns), HALF)] * 2
            + [pltpu.VMEM((2 * width, width), HALF)] * 2,
        ),
        compiler_params=pltpu.CompilerParams(vmem_limit_bytes=48 << 20),
        name="panel_products",
        cost_estimate=pl.CostEstimate(
            flops=3 * (4 * width * rows * columns + 12 * width * width * rows),
            bytes_accessed=4 * (rows * columns + 2 * width * columns + 3 * width * rows),
            transcendentals=0,
        ),
    )(place, small, uio, lower, trail, *pieces)


def finish_kernel(
    inner, small, lot, uol, lin, uin, ldo, udo, lio, uio, corner_out, top_out, left_out
):
    width = lin.shape[0]
    row = lax.broadcasted_iota(jnp.int32, (width, width), 0)
    column = lax.broadcasted_iota(jnp.int32, (width, width), 1)
    below = row > column
    g11, g12 = inner[:width, :width], inner[:width, width:]
    g21, g22 = inner[width:, :width], inner[width:, width:]
    lin_t, uin_t, lio_t, uio_t = lin[...].T, uin[...].T, lio[...].T, uio[...].T
    inside = jnp.where(below, exact(small[X_NEW], g11), exact(g11, small[Y_NEW]))
    corner = exact(exact(lin_t, inside), uin_t)
    top = exact(exact(lin_t, g12), uio_t) - exact(corner, small[U_PAIR])
    left = exact(lio_t, exact(g21, uin_t)) - exact(small[L_PAIR], corner)
    top_out[...] = top
    left_out[...] = left
    outer = exact(small[L_TRIPLE], g12) - exact(lio_t, g22)
    under = exact(g21, small[U_TRIPLE]) - exact(g22, uio_t)
    lower_grad = -(exact(left, uol[...].T) + outer)
    upper_grad = -(exact(lot[...].T, top) + under)
    inside = jnp.where(
        below, exact(ldo[...].T, lower_grad), exact(upper_grad, udo[...].T)
    )
    corner_out[...] = exact(exact(lio_t, inside), uio_t)


def finish(inner, small, *factors):
    width = factors[0].shape[0]
    return pl.pallas_call(
        finish_kernel,
        out_shape=(jax.ShapeDtypeStruct((width, width), FULL),) * 3,
        in_specs=[VMEM] * (2 + len(factors)),
        out_specs=(VMEM,) * 3,
        name="finish",
        cost_estimate=pl.CostEstimate(
            flops=240 * width**3, bytes_accessed=84 * width**2, transcendentals=0
        ),
    )(inner, small, *factors)


def swap(value, axis, step):
    size = lax.axis_size(axis)
    return lax.ppermute(value, axis, [(i, i ^ step) for i in range(size)])


def block(value, index, size):
    return lax.dynamic_slice_in_dim(value, index * size, size, 0)


def scatter_sum(value, axis):
    count = lax.axis_size(axis)
    me = lax.axis_index(axis)
    size = value.shape[0] // count
    total = block(value, me, size)
    for step in range(1, count):
        total = total + swap(block(value, me ^ step, size), axis, step)
    return total


def pieces_of(value, axis):
    return [value] + [swap(value, axis, step) for step in range(1, lax.axis_size(axis))]


def placed(pieces, axis):
    me = lax.axis_index(axis)
    size = pieces[0].shape[0]
    out = jnp.zeros((len(pieces) * size, *pieces[0].shape[1:]), pieces[0].dtype)
    for step, piece in enumerate(pieces):
        out = lax.dynamic_update_slice_in_dim(out, piece, (me ^ step) * size, 0)
    return out


def gather(value, axis):
    return placed(pieces_of(value, axis), axis)


def together(*values):
    return lax.optimization_barrier(values)


def total(value, axis):
    own, first, second, third = pieces_of(value, axis)
    return (own + first) + (second + third)


def body(
    trail,
    lower_new,
    upper_new,
    lot,
    lower_old,
    uol,
    upper_old,
    ldn,
    udn,
    lin,
    uin,
    ldo,
    udo,
    lio,
    uio,
):
    row, col = ("z", "y"), ("x", "c")
    count = lax.axis_size(col)
    ranks = lax.axis_size(row)

    lower_mine = jnp.concatenate((lower_new.T, lower_old.T), axis=0)
    lower_stack = lax.all_gather(lower_mine, col, axis=0, tiled=True)
    near = together(*pieces_of(upper_new, "z"), *pieces_of(upper_old, "y"))
    near_new, near_old = together(placed(near[:4], "z"), placed(near[4:], "y"))
    pieces = pieces_of(near_new, "y") + pieces_of(near_old, "z")

    small = prepare(lot, uol, ldn, udn, lin, uin, lio, uio)
    band = band_products(small, lio, lower_stack, trail, ranks, count)
    *pieces, _ = together(*pieces, band)
    band = lax.all_to_all(band, row, 0, 0, tiled=True)

    place = jnp.stack((lax.axis_index("z"), lax.axis_index("y"))).astype(jnp.int32)
    inner, strip = panel_products(place, small, uio, lower_stack, trail, pieces, count)
    strip_bottom = lax.psum_scatter(strip, col, scatter_dimension=0, tiled=True)

    inner = scatter_sum(scatter_sum(inner, "c"), "x")
    inner, band = together(inner, band.sum(0))
    half = band.shape[0] // 2
    first = pieces_of(band[:half], "y")
    second = pieces_of(band[half:], "z")
    inner = total(total(inner, "y"), "z")
    inner, *band = together(inner, *first, *second)
    first = pieces_of(placed(band[:4], "y"), "z")
    second = pieces_of(placed(band[4:], "z"), "y")
    inner, strip_bottom = together(inner, strip_bottom)
    inner = gather(gather(inner, "x"), "c")
    small_outs = finish(inner, small, lot, uol, lin, uin, ldo, udo, lio, uio)
    *band, corner_old, strip_top, band_left = together(*first, *second, *small_outs)
    band_right = jnp.concatenate((placed(band[:4], "z"), placed(band[4:], "y")), axis=0)
    return corner_old, strip_top, strip_bottom, band_left, band_right


def solution(mesh):
    fine = Mesh(mesh.devices.reshape(4, 4, 4, 2), ("z", "y", "x", "c"))
    row, col = ("z", "y"), ("x", "c")
    split, whole = P(row, col), P()
    return jax.shard_map(
        body,
        mesh=fine,
        in_specs=(split, split, split, whole, split, whole, split) + (whole,) * 8,
        out_specs=(whole, whole, P(row + col, None), whole, P(None, col)),
        check_vma=False,
    )
```

```python
import functools

import jax
import jax.numpy as jnp
from jax import lax
from jax.experimental import pallas as pl
from jax.experimental.pallas import tpu as pltpu
from jax.sharding import Mesh, PartitionSpec as P

HALF = jnp.bfloat16
FULL = jnp.float32
VMEM = pl.BlockSpec(memory_space=pltpu.VMEM)


def mul(left, right, dims):
    return lax.dot_general(left, right, (dims, ((), ())), preferred_element_type=FULL)


def parts(value):
    high = value.astype(HALF)
    return high, (value - high.astype(FULL)).astype(HALF)


def close(left, right, dims=((1,), (0,))):
    (lh, ll), (rh, rl) = left, right
    return mul(lh, rl, dims) + mul(ll, rh, dims) + mul(lh, rh, dims)


def times(left, right):
    return close(parts(left), parts(right))


def far(*arrays):
    return [pltpu.with_memory_space_constraint(a, pltpu.HBM) for a in arrays]


X_NEW, Y_NEW, U_PAIR, U_TRIPLE, L_PAIR, L_TRIPLE = range(6)


def prepare_kernel(lot, uol, ldn, udn, lin, uin, lio, uio, out):
    upper_pair = times(uol[...].T, uio[...].T)
    lower_pair = times(lio[...].T, lot[...].T)
    out[X_NEW] = times(ldn[...].T, lin[...].T)
    out[Y_NEW] = times(uin[...].T, udn[...].T)
    out[U_PAIR] = upper_pair
    out[L_PAIR] = lower_pair
    out[U_TRIPLE] = times(uin[...].T, upper_pair)
    out[L_TRIPLE] = times(lower_pair, lin[...].T)


def prepare(*factors):
    width = factors[0].shape[0]
    return pl.pallas_call(
        prepare_kernel,
        out_shape=jax.ShapeDtypeStruct((6, width, width), FULL),
        in_specs=[VMEM] * len(factors),
        out_specs=VMEM,
        name="prepare",
        cost_estimate=pl.CostEstimate(
            flops=72 * width**3, bytes_accessed=56 * width**2, transcendentals=0
        ),
    )(*factors)


def lower_rows(lower, panel, count, piece):
    return jnp.concatenate(
        [
            lower[pl.ds((2 * k + panel) * piece, piece), :]
            for k in range(count)
        ],
        axis=0,
    )


def band_kernel(count, small, lio, lower, trail, out, weight_high, weight_low):
    width = lio.shape[0]
    piece = width // count

    @pl.when(pl.program_id(0) == 0)
    def _():
        new = parts(lower_rows(lower, 0, count, piece))
        old = parts(lower_rows(lower, 1, count, piece))
        weight = close(parts(small[0]), new) - close(parts(lio[...].T), old)
        high, low = parts(weight)
        weight_high[...] = high
        weight_low[...] = low

    band = close((weight_high[...], weight_low[...]), parts(trail[...]))
    size = out.shape[1]
    for k in range(out.shape[0]):
        out[k] = band[k * size : (k + 1) * size, :]


def band_products(small, lio, lower, trail, ranks, count, tile=512):
    rows, columns = trail.shape
    width = lio.shape[0]
    small, lio, lower, trail = far(small, lio, lower, trail)
    return pl.pallas_call(
        functools.partial(band_kernel, count),
        out_shape=jax.ShapeDtypeStruct((ranks, width // ranks, columns), FULL),
        grid=(columns // tile,),
        in_specs=[
            pl.BlockSpec((1, width, width), lambda j: (L_TRIPLE, 0, 0)),
            pl.BlockSpec((width, width), lambda j: (0, 0)),
            pl.BlockSpec((2 * width, rows), lambda j: (0, 0)),
            pl.BlockSpec((rows, tile), lambda j: (0, j)),
        ],
        out_specs=pl.BlockSpec((ranks, width // ranks, tile), lambda j: (0, 0, j)),
        scratch_shapes=[pltpu.VMEM((width, rows), HALF)] * 2,
        compiler_params=pltpu.CompilerParams(vmem_limit_bytes=24 << 20),
        name="band_products",
        cost_estimate=pl.CostEstimate(
            flops=6 * width * rows * columns,
            bytes_accessed=4 * (rows * columns + 2 * width * rows + width * columns),
            transcendentals=0,
        ),
    )(small, lio, lower, trail)


def panel_kernel(count, place, small, uio, lower, trail, *rest):
    pieces = rest[:8]
    mine, other, strip_out, upper_high, upper_low, side_high, side_low, inner = rest[8:]
    width = uio.shape[0]
    z, y, x, c = place[0], place[1], place[2], place[3]

    @pl.when(pl.program_id(0) == 0)
    def _():
        inner[...] = jnp.zeros_like(inner)
        high, low = parts(small[0])
        side_high[:width, :] = high
        side_low[:width, :] = low
        high, low = parts(-uio[...].T)
        side_high[width:, :] = high
        side_low[width:, :] = low
        for k in range(4):
            high, low = parts(pieces[k][...])
            chunk = high.shape[0] // 4
            for zz in range(4):
                at = pl.ds(pl.multiple_of((4 * zz + (y ^ k)) * chunk, chunk), chunk)
                upper_high[at, :] = high[zz * chunk : (zz + 1) * chunk, :]
                upper_low[at, :] = low[zz * chunk : (zz + 1) * chunk, :]
            high, low = parts(pieces[4 + k][...])
            size = high.shape[0]
            at = pl.ds(pl.multiple_of(width + (z ^ k) * size, size), size)
            upper_high[at, :] = high
            upper_low[at, :] = low

    product = close(parts(trail[...]), (upper_high[...], upper_low[...]), ((1,), (1,)))
    product = parts(product)
    strip = close(product, (side_high[...], side_low[...]))
    strip_out[...] = strip
    piece = width // count
    for panel in range(2):
        left = parts(lower_rows(lower, panel, count, piece))
        inner[panel * width : (panel + 1) * width, :] += close(left, product)

    @pl.when(pl.program_id(0) == pl.num_programs(0) - 1)
    def _():
        rows, share = mine.shape[2], width // 4
        for k in range(4):
            for p in range(mine.shape[1]):
                start, column = (x ^ k) * share + rows * (p // 2), width * (p % 2)
                near = pl.ds(pl.multiple_of(c * width + start, rows), rows)
                beside = pl.ds(pl.multiple_of((1 - c) * width + start, rows), rows)
                mine[k, p] = inner[near, column : column + width]
                other[k, p] = inner[beside, column : column + width]


def panel_products(place, small, uio, lower, trail, pieces, count, tile=256):
    rows, columns = trail.shape
    width = uio.shape[0]
    once = pl.Buffered(1)
    size = pieces[0].shape[0]
    share = (4, 16, width // 32, width)
    small, uio, lower, trail = far(small, uio, lower, trail)
    return pl.pallas_call(
        functools.partial(panel_kernel, count),
        out_shape=(
            jax.ShapeDtypeStruct(share, FULL),
            jax.ShapeDtypeStruct(share, FULL),
            jax.ShapeDtypeStruct((rows, width), FULL),
        ),
        grid_spec=pltpu.PrefetchScalarGridSpec(
            num_scalar_prefetch=1,
            grid=(rows // tile,),
            in_specs=[
                pl.BlockSpec((1, width, width), lambda i, p: (U_TRIPLE, 0, 0)),
                pl.BlockSpec((width, width), lambda i, p: (0, 0)),
                pl.BlockSpec((2 * width, tile), lambda i, p: (0, i)),
                pl.BlockSpec((tile, columns), lambda i, p: (i, 0)),
            ]
            + [pl.BlockSpec((size, columns), lambda i, p: (0, 0), pipeline_mode=once)] * 8,
            out_specs=(
                pl.BlockSpec(share, lambda i, p: (0, 0, 0, 0)),
                pl.BlockSpec(share, lambda i, p: (0, 0, 0, 0)),
                pl.BlockSpec((tile, width), lambda i, p: (i, 0)),
            ),
            scratch_shapes=[pltpu.VMEM((2 * width, columns), HALF)] * 2
            + [pltpu.VMEM((2 * width, width), HALF)] * 2
            + [pltpu.VMEM((2 * width, 2 * width), FULL)],
        ),
        compiler_params=pltpu.CompilerParams(vmem_limit_bytes=36 << 20),
        name="panel_products",
        cost_estimate=pl.CostEstimate(
            flops=3 * (4 * width * rows * columns + 12 * width * width * rows),
            bytes_accessed=4 * (rows * columns + 2 * width * columns + 4 * width * rows),
            transcendentals=0,
        ),
    )(place, small, uio, lower, trail, *pieces)


def finish_kernel(
    place,
    mine,
    other,
    small,
    lot,
    uol,
    lin,
    uin,
    ldo,
    udo,
    lio,
    uio,
    corner_out,
    top_out,
    left_out,
    inner,
):
    width = lin.shape[0]
    c = place[3]
    rows, share = mine.shape[2], width // 4
    for k in range(4):
        for p in range(mine.shape[1]):
            start, column = k * share + rows * (p // 2), width * (p % 2)
            near = pl.ds(pl.multiple_of(c * width + start, rows), rows)
            beside = pl.ds(pl.multiple_of((1 - c) * width + start, rows), rows)
            inner[near, column : column + width] = mine[k, p]
            inner[beside, column : column + width] = other[k, p]
    row = lax.broadcasted_iota(jnp.int32, (width, width), 0)
    column = lax.broadcasted_iota(jnp.int32, (width, width), 1)
    below = row > column
    g11, g12 = inner[:width, :width], inner[:width, width:]
    g21, g22 = inner[width:, :width], inner[width:, width:]
    lin_t, uin_t, lio_t, uio_t = lin[...].T, uin[...].T, lio[...].T, uio[...].T
    inside = jnp.where(below, times(small[X_NEW], g11), times(g11, small[Y_NEW]))
    corner = times(times(lin_t, inside), uin_t)
    top = times(times(lin_t, g12), uio_t) - times(corner, small[U_PAIR])
    left = times(lio_t, times(g21, uin_t)) - times(small[L_PAIR], corner)
    top_out[...] = top
    left_out[...] = left
    outer = times(small[L_TRIPLE], g12) - times(lio_t, g22)
    under = times(g21, small[U_TRIPLE]) - times(g22, uio_t)
    lower_grad = -(times(left, uol[...].T) + outer)
    upper_grad = -(times(lot[...].T, top) + under)
    inside = jnp.where(
        below, times(ldo[...].T, lower_grad), times(upper_grad, udo[...].T)
    )
    corner_out[...] = times(times(lio_t, inside), uio_t)


def finish(place, mine, other, small, *factors):
    width = factors[0].shape[0]
    return pl.pallas_call(
        finish_kernel,
        out_shape=(jax.ShapeDtypeStruct((width, width), FULL),) * 3,
        in_specs=[pl.BlockSpec(memory_space=pltpu.SMEM)] + [VMEM] * (3 + len(factors)),
        out_specs=(VMEM,) * 3,
        scratch_shapes=[pltpu.VMEM((2 * width, 2 * width), FULL)],
        name="finish",
        cost_estimate=pl.CostEstimate(
            flops=240 * width**3, bytes_accessed=84 * width**2, transcendentals=0
        ),
    )(place, mine, other, small, *factors)


def swap(value, axis, step):
    size = lax.axis_size(axis)
    return lax.ppermute(value, axis, [(i, i ^ step) for i in range(size)])


def exchange(value, axes):
    return lax.all_to_all(value, axes, 0, 0, tiled=True)


def pieces_of(value, axis):
    return [value] + [swap(value, axis, step) for step in range(1, lax.axis_size(axis))]


def placed(pieces, axis):
    me = lax.axis_index(axis)
    size = pieces[0].shape[0]
    out = jnp.zeros((len(pieces) * size, *pieces[0].shape[1:]), pieces[0].dtype)
    for step, piece in enumerate(pieces):
        out = lax.dynamic_update_slice_in_dim(out, piece, (me ^ step) * size, 0)
    return out


def together(*values):
    return lax.optimization_barrier(values)


def body(
    trail,
    lower_new,
    upper_new,
    lot,
    lower_old,
    uol,
    upper_old,
    ldn,
    udn,
    lin,
    uin,
    ldo,
    udo,
    lio,
    uio,
):
    row, col = ("z", "y"), ("x", "c")
    count = lax.axis_size(col)
    ranks = lax.axis_size(row)

    lower_mine = jnp.concatenate((lower_new.T, lower_old.T), axis=0)
    lower_stack = lax.all_gather(lower_mine, col, axis=0, tiled=True)
    small = prepare(lot, uol, ldn, udn, lin, uin, lio, uio)
    *near, small = together(*pieces_of(upper_new, "z"), *pieces_of(upper_old, "y"), small)
    near_new, near_old = together(placed(near[:4], "z"), placed(near[4:], "y"))
    pieces = pieces_of(near_new, "y") + pieces_of(near_old, "z")

    band = band_products(small, lio, lower_stack, trail, ranks, count)
    *pieces, _ = together(*pieces, band)
    band = lax.all_to_all(band, row, 0, 0, tiled=True)

    place = jnp.stack([lax.axis_index(a) for a in row + col]).astype(jnp.int32)
    mine, other, strip = panel_products(
        place, small, uio, lower_stack, trail, pieces, count
    )
    mine = mine + swap(other, "c", 1)
    mine = mine[0] + sum(swap(mine[k], "x", k) for k in (1, 2, 3))
    mine, band = together(mine, band.sum(0))
    band_right = lax.all_gather(band, row, axis=0, tiled=True)
    mine = exchange(mine, row).sum(0)
    mine = exchange(jnp.broadcast_to(mine[None], (ranks, *mine.shape)), row)
    mine = exchange(jnp.broadcast_to(mine[None], (4, *mine.shape)), "x")
    mine, strip = together(mine, strip)
    strip = exchange(strip.reshape(count, -1, strip.shape[1]), col)
    other = swap(mine, "c", 1)
    corner_old, strip_top, band_left = finish(
        place, mine, other, small, lot, uol, lin, uin, ldo, udo, lio, uio
    )
    strip_bottom, corner_old = together(strip, corner_old)
    return corner_old, strip_top, strip_bottom.sum(0), band_left, band_right


def solution(mesh):
    fine = Mesh(mesh.devices.reshape(4, 4, 4, 2), ("z", "y", "x", "c"))
    row, col = ("z", "y"), ("x", "c")
    split, whole = P(row, col), P()
    return jax.shard_map(
        body,
        mesh=fine,
        in_specs=(split, split, split, whole, split, whole, split) + (whole,) * 8,
        out_specs=(whole, whole, P(row + col, None), whole, P(None, col)),
        check_vma=False,
    )
```

```python
import functools

import jax
import jax.numpy as jnp
from jax import lax
from jax.experimental import pallas as pl
from jax.experimental.pallas import tpu as pltpu
from jax.sharding import Mesh, PartitionSpec as P

HALF = jnp.bfloat16
FULL = jnp.float32
VMEM = pl.BlockSpec(memory_space=pltpu.VMEM)


def mul(left, right, dims):
    return lax.dot_general(left, right, (dims, ((), ())), preferred_element_type=FULL)


def parts(value):
    high = value.astype(HALF)
    return high, (value - high.astype(FULL)).astype(HALF)


def close(left, right, dims=((1,), (0,))):
    (lh, ll), (rh, rl) = left, right
    return mul(lh, rl, dims) + mul(ll, rh, dims) + mul(lh, rh, dims)


def times(left, right):
    return close(parts(left), parts(right))


def far(*arrays):
    return [pltpu.with_memory_space_constraint(a, pltpu.HBM) for a in arrays]


def prepare_kernel(lot, uol, ldn, udn, lin, uin, lio, uio, *out):
    x_new, y_new, upper_pair, upper_triple, lower_pair, lower_triple = out
    upper = times(uol[...].T, uio[...].T)
    lower = times(lio[...].T, lot[...].T)
    x_new[...] = times(ldn[...].T, lin[...].T)
    y_new[...] = times(uin[...].T, udn[...].T)
    upper_pair[...] = upper
    lower_pair[...] = lower
    upper_triple[...] = times(uin[...].T, upper)
    lower_triple[...] = times(lower, lin[...].T)


def prepare(*factors):
    width = factors[0].shape[0]
    return pl.pallas_call(
        prepare_kernel,
        out_shape=(jax.ShapeDtypeStruct((width, width), FULL),) * 6,
        in_specs=[VMEM] * len(factors),
        out_specs=(VMEM,) * 6,
        name="prepare",
        cost_estimate=pl.CostEstimate(
            flops=36 * width**3, bytes_accessed=56 * width**2, transcendentals=0
        ),
    )(*factors)


def lower_rows(lower, panel, count, piece):
    return jnp.concatenate(
        [
            lower[pl.ds((2 * k + panel) * piece, piece), :]
            for k in range(count)
        ],
        axis=0,
    )


def weight_kernel(count, triple, lio, lower, high, low):
    piece = lio.shape[0] // count
    new = parts(lower_rows(lower, 0, count, piece))
    old = parts(lower_rows(lower, 1, count, piece))
    high[...], low[...] = parts(close(parts(triple[...]), new) - close(parts(lio[...].T), old))


def band_weights(triple, lio, lower, count):
    width, rows = lio.shape[0], lower.shape[1]
    return pl.pallas_call(
        functools.partial(weight_kernel, count),
        out_shape=(jax.ShapeDtypeStruct((width, rows), HALF),) * 2,
        in_specs=[VMEM] * 3,
        out_specs=(VMEM,) * 2,
        compiler_params=pltpu.CompilerParams(vmem_limit_bytes=16 << 20),
        name="band_weights",
        cost_estimate=pl.CostEstimate(
            flops=12 * width * width * rows,
            bytes_accessed=12 * width * rows,
            transcendentals=0,
        ),
    )(triple, lio, lower)


def band_kernel(high, low, trail, out):
    size = out.shape[1]
    band = close((high[...], low[...]), parts(trail[...]))
    for k in range(out.shape[0]):
        out[k] = band[k * size : (k + 1) * size, :]


def band_products(high, low, trail, ranks, tile=256):
    rows, columns = trail.shape
    width = high.shape[0]
    once = pl.BlockSpec((width, rows), lambda j: (0, 0), pipeline_mode=pl.Buffered(1))
    (trail,) = far(trail)
    return pl.pallas_call(
        band_kernel,
        out_shape=jax.ShapeDtypeStruct((ranks, width // ranks, columns), FULL),
        grid=(columns // tile,),
        in_specs=[once, once, pl.BlockSpec((rows, tile), lambda j: (0, j))],
        out_specs=pl.BlockSpec((ranks, width // ranks, tile), lambda j: (0, 0, j)),
        compiler_params=pltpu.CompilerParams(vmem_limit_bytes=20 << 20),
        name="band_products",
        cost_estimate=pl.CostEstimate(
            flops=6 * width * rows * columns,
            bytes_accessed=4 * (rows * columns + width * rows + width * columns),
            transcendentals=0,
        ),
    )(high, low, trail)


def panel_kernel(count, tile, place, triple, uio, lower, trail, *rest):
    pieces = rest[:8]
    mine, other, strip, upper_high, upper_low, side_high, side_low, inner = rest[8:]
    width = uio.shape[0]
    z, y, x, c = place[0], place[1], place[2], place[3]
    piece = width // count

    def assemble():
        inner[...] = jnp.zeros_like(inner)
        side_high[:width, :], side_low[:width, :] = parts(triple[...])
        side_high[width:, :], side_low[width:, :] = parts(-uio[...].T)
        chunk = pieces[0].shape[0] // 4
        for k in range(8):
            for q in range(4):
                rank = 4 * (z ^ (k - 4)) + q if k >= 4 else 4 * q + (y ^ k)
                start = (k // 4) * width + rank * chunk
                at = pl.ds(pl.multiple_of(start, chunk), chunk)
                upper_high[at, :], upper_low[at, :] = parts(
                    pieces[k][q * chunk : (q + 1) * chunk, :]
                )

    def step(lower_tile, trail_tile, strip_tile):
        pl.when(pl.program_id(0) == 0)(assemble)
        product = close(
            parts(trail_tile[...]), (upper_high[...], upper_low[...]), ((1,), (1,))
        )
        product = parts(product)
        strip_tile[...] = close(product, (side_high[...], side_low[...]))
        for panel in range(2):
            left = parts(lower_rows(lower_tile, panel, count, piece))
            inner[panel * width : (panel + 1) * width, :] += close(left, product)

    pltpu.emit_pipeline(
        step,
        grid=(trail.shape[0] // tile,),
        in_specs=[
            pl.BlockSpec((lower.shape[0], tile), lambda i: (0, i)),
            pl.BlockSpec((tile, trail.shape[1]), lambda i: (i, 0)),
        ],
        out_specs=[pl.BlockSpec((tile, width), lambda i: (i, 0))],
    )(lower, trail, strip)

    rows, share = mine.shape[2], width // 4
    for k in range(4):
        for p in range(mine.shape[1]):
            start, column = (x ^ k) * share + rows * (p // 2), width * (p % 2)
            near = pl.ds(pl.multiple_of(c * width + start, rows), rows)
            beside = pl.ds(pl.multiple_of((1 - c) * width + start, rows), rows)
            mine[k, p] = inner[near, column : column + width]
            other[k, p] = inner[beside, column : column + width]


def panel_products(place, triple, uio, lower, trail, pieces, count, tile=256):
    rows, columns = trail.shape
    width = uio.shape[0]
    share = (4, 16, width // 32, width)
    lower, trail = far(lower, trail)
    hbm = pl.BlockSpec(memory_space=pltpu.HBM)
    return pl.pallas_call(
        functools.partial(panel_kernel, count, tile),
        out_shape=(
            jax.ShapeDtypeStruct(share, FULL),
            jax.ShapeDtypeStruct(share, FULL),
            jax.ShapeDtypeStruct((rows, width), FULL),
        ),
        in_specs=[pl.BlockSpec(memory_space=pltpu.SMEM), VMEM, VMEM, hbm, hbm] + [VMEM] * 8,
        out_specs=(VMEM, VMEM, hbm),
        scratch_shapes=[pltpu.VMEM((2 * width, columns), HALF)] * 2
        + [pltpu.VMEM((2 * width, width), HALF)] * 2
        + [pltpu.VMEM((2 * width, 2 * width), FULL)],
        compiler_params=pltpu.CompilerParams(vmem_limit_bytes=36 << 20),
        name="panel_products",
        cost_estimate=pl.CostEstimate(
            flops=3 * (4 * width * rows * columns + 12 * width * width * rows),
            bytes_accessed=4 * (rows * columns + 2 * width * columns + 4 * width * rows),
            transcendentals=0,
        ),
    )(place, triple, uio, lower, trail, *pieces)


def finish_kernel(
    place,
    mine,
    other,
    x_new,
    y_new,
    upper_pair,
    upper_triple,
    lower_pair,
    lower_triple,
    lot,
    uol,
    lin,
    uin,
    ldo,
    udo,
    lio,
    uio,
    corner_out,
    top_out,
    left_out,
    inner,
):
    width = lin.shape[0]
    c = place[3]
    rows, share = mine.shape[2], width // 4
    for k in range(4):
        for p in range(mine.shape[1]):
            start, column = k * share + rows * (p // 2), width * (p % 2)
            near = pl.ds(pl.multiple_of(c * width + start, rows), rows)
            beside = pl.ds(pl.multiple_of((1 - c) * width + start, rows), rows)
            inner[near, column : column + width] = mine[k, p]
            inner[beside, column : column + width] = other[k, p]
    row = lax.broadcasted_iota(jnp.int32, (width, width), 0)
    column = lax.broadcasted_iota(jnp.int32, (width, width), 1)
    below = row > column
    g11, g12 = inner[:width, :width], inner[:width, width:]
    g21, g22 = inner[width:, :width], inner[width:, width:]
    lin_t, uin_t, lio_t, uio_t = lin[...].T, uin[...].T, lio[...].T, uio[...].T
    inside = jnp.where(below, times(x_new[...], g11), times(g11, y_new[...]))
    corner = times(times(lin_t, inside), uin_t)
    top = times(times(lin_t, g12), uio_t) - times(corner, upper_pair[...])
    left = times(lio_t, times(g21, uin_t)) - times(lower_pair[...], corner)
    top_out[...] = top
    left_out[...] = left
    outer = times(lower_triple[...], g12) - times(lio_t, g22)
    under = times(g21, upper_triple[...]) - times(g22, uio_t)
    lower_grad = -(times(left, uol[...].T) + outer)
    upper_grad = -(times(lot[...].T, top) + under)
    inside = jnp.where(
        below, times(ldo[...].T, lower_grad), times(upper_grad, udo[...].T)
    )
    corner_out[...] = times(times(lio_t, inside), uio_t)


def finish(place, mine, other, *factors):
    width = factors[0].shape[0]
    mine, other = (pltpu.with_memory_space_constraint(a, pltpu.VMEM) for a in (mine, other))
    return pl.pallas_call(
        finish_kernel,
        out_shape=(jax.ShapeDtypeStruct((width, width), FULL),) * 3,
        in_specs=[pl.BlockSpec(memory_space=pltpu.SMEM)] + [VMEM] * (2 + len(factors)),
        out_specs=(VMEM,) * 3,
        scratch_shapes=[pltpu.VMEM((2 * width, 2 * width), FULL)],
        name="finish",
        cost_estimate=pl.CostEstimate(
            flops=240 * width**3, bytes_accessed=84 * width**2, transcendentals=0
        ),
    )(place, mine, other, *factors)


def swap(value, axis, step):
    size = lax.axis_size(axis)
    return lax.ppermute(value, axis, [(i, i ^ step) for i in range(size)])


def exchange(value, axes):
    return lax.all_to_all(value, axes, 0, 0, tiled=True)


def pieces_of(value, axis):
    return [value] + [swap(value, axis, step) for step in range(1, lax.axis_size(axis))]


def placed(pieces, axis):
    me = lax.axis_index(axis)
    size = pieces[0].shape[0]
    out = jnp.zeros((len(pieces) * size, *pieces[0].shape[1:]), pieces[0].dtype)
    for step, piece in enumerate(pieces):
        out = lax.dynamic_update_slice_in_dim(out, piece, (me ^ step) * size, 0)
    return out


def together(*values):
    return lax.optimization_barrier(values)


def body(
    trail,
    lower_new,
    upper_new,
    lot,
    lower_old,
    uol,
    upper_old,
    ldn,
    udn,
    lin,
    uin,
    ldo,
    udo,
    lio,
    uio,
):
    row, col = ("z", "y"), ("x", "c")
    count = lax.axis_size(col)
    ranks = lax.axis_size(row)

    lower_mine = jnp.concatenate((lower_new.T, lower_old.T), axis=0)
    lower_stack = lax.all_gather(lower_mine, col, axis=0, tiled=True)
    small = prepare(lot, uol, ldn, udn, lin, uin, lio, uio)
    *near, small = together(*pieces_of(upper_new, "z"), *pieces_of(upper_old, "y"), small)
    near_new, near_old = together(placed(near[:4], "z"), placed(near[4:], "y"))
    upper_triple, lower_triple = small[3], small[5]
    weights = band_weights(lower_triple, lio, lower_stack, count)
    pieces = pieces_of(near_new, "y") + [near_old, swap(near_old, "z", 1), swap(near_old, "z", 2)]
    last, weights = together(near_old, weights)
    pieces.append(swap(last, "z", 3))

    band = band_products(*weights, trail, ranks)
    *pieces, _ = together(*pieces, band)
    band = lax.all_to_all(band, row, 0, 0, tiled=True)

    place = jnp.stack([lax.axis_index(a) for a in row + col]).astype(jnp.int32)
    mine, other, strip = panel_products(
        place, upper_triple, uio, lower_stack, trail, pieces, count
    )
    mine = mine + swap(other, "c", 1)
    mine = mine[0] + sum(swap(mine[k], "x", k) for k in (1, 2, 3))
    mine, band = together(mine, band.sum(0))
    band_right = -lax.all_gather(-band, row, axis=0, tiled=True)
    mine = exchange(mine, row).sum(0)
    mine = exchange(jnp.broadcast_to(mine[None], (ranks, *mine.shape)), row)
    mine = exchange(jnp.broadcast_to(mine[None], (4, *mine.shape)), "x")
    mine, strip = together(mine, strip)
    strip = exchange(strip.reshape(count, -1, strip.shape[1]), col)
    other = swap(mine, "c", 1)
    corner_old, strip_top, band_left = finish(
        place, mine, other, *small, lot, uol, lin, uin, ldo, udo, lio, uio
    )
    strip, corner_old, band_right = together(strip, corner_old, band_right)
    return corner_old, strip_top, strip.sum(0), band_left, band_right


def solution(mesh):
    fine = Mesh(mesh.devices.reshape(4, 4, 4, 2), ("z", "y", "x", "c"))
    row, col = ("z", "y"), ("x", "c")
    split, whole = P(row, col), P()
    return jax.shard_map(
        body,
        mesh=fine,
        in_specs=(split, split, split, whole, split, whole, split) + (whole,) * 8,
        out_specs=(whole, whole, P(row + col, None), whole, P(None, col)),
        check_vma=False,
    )
```

```python
import functools

import jax
import jax.numpy as jnp
from jax import lax
from jax.experimental import pallas as pl
from jax.experimental.pallas import tpu as pltpu
from jax.sharding import Mesh, PartitionSpec as P

HALF = jnp.bfloat16
FULL = jnp.float32
VMEM = pl.BlockSpec(memory_space=pltpu.VMEM)


def mul(left, right, dims):
    return lax.dot_general(left, right, (dims, ((), ())), preferred_element_type=FULL)


def parts(value):
    high = value.astype(HALF)
    return high, (value - high.astype(FULL)).astype(HALF)


def close(left, right, dims=((1,), (0,))):
    (lh, ll), (rh, rl) = left, right
    return mul(lh, rl, dims) + mul(ll, rh, dims) + mul(lh, rh, dims)


def times(left, right):
    return close(parts(left), parts(right))


def far(*arrays):
    return [pltpu.with_memory_space_constraint(a, pltpu.HBM) for a in arrays]


def prepare_kernel(lot, uol, ldn, udn, lin, uin, lio, uio, *out):
    x_new, y_new, upper_pair, upper_triple, lower_pair, lower_triple = out
    upper = times(uol[...].T, uio[...].T)
    lower = times(lio[...].T, lot[...].T)
    x_new[...] = times(ldn[...].T, lin[...].T)
    y_new[...] = times(uin[...].T, udn[...].T)
    upper_pair[...] = upper
    lower_pair[...] = lower
    upper_triple[...] = times(uin[...].T, upper)
    lower_triple[...] = times(lower, lin[...].T)


def prepare(*factors):
    width = factors[0].shape[0]
    return pl.pallas_call(
        prepare_kernel,
        out_shape=(jax.ShapeDtypeStruct((width, width), FULL),) * 6,
        in_specs=[VMEM] * len(factors),
        out_specs=(VMEM,) * 6,
        name="prepare",
        cost_estimate=pl.CostEstimate(
            flops=36 * width**3, bytes_accessed=56 * width**2, transcendentals=0
        ),
    )(*factors)


def lower_rows(lower, panel, count, piece):
    return jnp.concatenate(
        [
            lower[pl.ds((2 * k + panel) * piece, piece), :]
            for k in range(count)
        ],
        axis=0,
    )


def band_kernel(count, triple, lio, lower, trail, out, weights):
    width = lio.shape[0]
    piece = width // count

    @pl.when(pl.program_id(0) == 0)
    def _():
        new = parts(lower_rows(lower, 0, count, piece))
        old = parts(lower_rows(lower, 1, count, piece))
        weight = close(parts(triple[...]), new) - close(parts(lio[...].T), old)
        weights[:width, :], weights[width:, :] = parts(weight)

    high, low = parts(trail[...])
    both = mul(weights[...], high, ((1,), (0,)))
    band = mul(weights[:width, :], low, ((1,), (0,))) + both[width:, :] + both[:width, :]
    size = out.shape[1]
    for k in range(out.shape[0]):
        out[k] = band[k * size : (k + 1) * size, :]


def band_products(triple, lio, lower, trail, ranks, count, tile=512):
    rows, columns = trail.shape
    width = lio.shape[0]
    once = pl.Buffered(1)
    triple, lio, lower, trail = far(triple, lio, lower, trail)
    return pl.pallas_call(
        functools.partial(band_kernel, count),
        out_shape=jax.ShapeDtypeStruct((ranks, width // ranks, columns), FULL),
        grid=(columns // tile,),
        in_specs=[
            pl.BlockSpec((width, width), lambda j: (0, 0), pipeline_mode=once),
            pl.BlockSpec((width, width), lambda j: (0, 0), pipeline_mode=once),
            pl.BlockSpec((2 * width, rows), lambda j: (0, 0), pipeline_mode=once),
            pl.BlockSpec((rows, tile), lambda j: (0, j)),
        ],
        out_specs=pl.BlockSpec((ranks, width // ranks, tile), lambda j: (0, 0, j)),
        scratch_shapes=[pltpu.VMEM((2 * width, rows), HALF)],
        compiler_params=pltpu.CompilerParams(vmem_limit_bytes=24 << 20),
        name="band_products",
        cost_estimate=pl.CostEstimate(
            flops=6 * width * rows * columns,
            bytes_accessed=4 * (rows * columns + 2 * width * rows + width * columns),
            transcendentals=0,
        ),
    )(triple, lio, lower, trail)


def panel_kernel(count, tile, place, triple, uio, lower, trail, *rest):
    pieces = rest[:8]
    mine, other, strip, upper_high, upper_low, side_high, side_low, inner = rest[8:]
    width = uio.shape[0]
    z, y, x, c = place[0], place[1], place[2], place[3]
    piece = width // count

    def assemble(triple, uio):
        inner[...] = jnp.zeros_like(inner)
        side_high[:width, :], side_low[:width, :] = parts(triple[...])
        side_high[width:, :], side_low[width:, :] = parts(-uio[...].T)
        chunk = pieces[0].shape[0] // 4
        for k in range(8):
            for q in range(4):
                rank = 4 * (z ^ (k - 4)) + q if k >= 4 else 4 * q + (y ^ k)
                start = (k // 4) * width + rank * chunk
                at = pl.ds(pl.multiple_of(start, chunk), chunk)
                upper_high[at, :], upper_low[at, :] = parts(
                    pieces[k][q * chunk : (q + 1) * chunk, :]
                )

    def step(triple_here, uio_here, lower_tile, trail_tile, strip_tile):
        @pl.when(pl.program_id(0) == 0)
        def _():
            assemble(triple_here, uio_here)

        product = close(
            parts(trail_tile[...]), (upper_high[...], upper_low[...]), ((1,), (1,))
        )
        product = parts(product)
        strip_tile[...] = close(product, (side_high[...], side_low[...]))
        for panel in range(2):
            left = parts(lower_rows(lower_tile, panel, count, piece))
            inner[panel * width : (panel + 1) * width, :] += close(left, product)

    pltpu.emit_pipeline(
        step,
        grid=(trail.shape[0] // tile,),
        in_specs=[
            pl.BlockSpec((width, width), lambda i: (0, 0)),
            pl.BlockSpec((width, width), lambda i: (0, 0)),
            pl.BlockSpec((lower.shape[0], tile), lambda i: (0, i)),
            pl.BlockSpec((tile, trail.shape[1]), lambda i: (i, 0)),
        ],
        out_specs=[pl.BlockSpec((tile, width), lambda i: (i, 0))],
    )(triple, uio, lower, trail, strip)

    rows, share = mine.shape[2], width // 4
    for k in range(4):
        for p in range(mine.shape[1]):
            start, column = (x ^ k) * share + rows * (p // 2), width * (p % 2)
            near = pl.ds(pl.multiple_of(c * width + start, rows), rows)
            beside = pl.ds(pl.multiple_of((1 - c) * width + start, rows), rows)
            mine[k, p] = inner[near, column : column + width]
            other[k, p] = inner[beside, column : column + width]


def panel_products(place, triple, uio, lower, trail, pieces, count, tile=256):
    rows, columns = trail.shape
    width = uio.shape[0]
    share = (4, 16, width // 32, width)
    triple, uio, lower, trail = far(triple, uio, lower, trail)
    hbm = pl.BlockSpec(memory_space=pltpu.HBM)
    return pl.pallas_call(
        functools.partial(panel_kernel, count, tile),
        out_shape=(
            jax.ShapeDtypeStruct(share, FULL),
            jax.ShapeDtypeStruct(share, FULL),
            jax.ShapeDtypeStruct((rows, width), FULL),
        ),
        in_specs=[pl.BlockSpec(memory_space=pltpu.SMEM)] + [hbm] * 4 + [VMEM] * 8,
        out_specs=(VMEM, VMEM, hbm),
        scratch_shapes=[pltpu.VMEM((2 * width, columns), HALF)] * 2
        + [pltpu.VMEM((2 * width, width), HALF)] * 2
        + [pltpu.VMEM((2 * width, 2 * width), FULL)],
        compiler_params=pltpu.CompilerParams(vmem_limit_bytes=36 << 20),
        name="panel_products",
        cost_estimate=pl.CostEstimate(
            flops=3 * (4 * width * rows * columns + 12 * width * width * rows),
            bytes_accessed=4 * (rows * columns + 2 * width * columns + 4 * width * rows),
            transcendentals=0,
        ),
    )(place, triple, uio, lower, trail, *pieces)


def finish_kernel(
    place,
    mine,
    other,
    x_new,
    y_new,
    upper_pair,
    upper_triple,
    lower_pair,
    lower_triple,
    lot,
    uol,
    lin,
    uin,
    ldo,
    udo,
    lio,
    uio,
    corner_out,
    top_out,
    left_out,
    inner,
):
    width = lin.shape[0]
    c = place[3]
    rows, share = mine.shape[2], width // 4
    for k in range(4):
        for p in range(mine.shape[1]):
            start, column = k * share + rows * (p // 2), width * (p % 2)
            near = pl.ds(pl.multiple_of(c * width + start, rows), rows)
            beside = pl.ds(pl.multiple_of((1 - c) * width + start, rows), rows)
            inner[near, column : column + width] = mine[k, p]
            inner[beside, column : column + width] = other[k, p]
    row = lax.broadcasted_iota(jnp.int32, (width, width), 0)
    column = lax.broadcasted_iota(jnp.int32, (width, width), 1)
    below = row > column
    g11, g12 = inner[:width, :width], inner[:width, width:]
    g21, g22 = inner[width:, :width], inner[width:, width:]
    lin_t, uin_t, lio_t, uio_t = lin[...].T, uin[...].T, lio[...].T, uio[...].T
    inside = jnp.where(below, times(x_new[...], g11), times(g11, y_new[...]))
    corner = times(times(lin_t, inside), uin_t)
    top = times(times(lin_t, g12), uio_t) - times(corner, upper_pair[...])
    left = times(lio_t, times(g21, uin_t)) - times(lower_pair[...], corner)
    top_out[...] = top
    left_out[...] = left
    outer = times(lower_triple[...], g12) - times(lio_t, g22)
    under = times(g21, upper_triple[...]) - times(g22, uio_t)
    lower_grad = -(times(left, uol[...].T) + outer)
    upper_grad = -(times(lot[...].T, top) + under)
    inside = jnp.where(
        below, times(ldo[...].T, lower_grad), times(upper_grad, udo[...].T)
    )
    corner_out[...] = times(times(lio_t, inside), uio_t)


def finish(place, mine, other, *factors):
    width = factors[0].shape[0]
    mine, other = (pltpu.with_memory_space_constraint(a, pltpu.VMEM) for a in (mine, other))
    return pl.pallas_call(
        finish_kernel,
        out_shape=(jax.ShapeDtypeStruct((width, width), FULL),) * 3,
        in_specs=[pl.BlockSpec(memory_space=pltpu.SMEM)] + [VMEM] * (2 + len(factors)),
        out_specs=(VMEM,) * 3,
        scratch_shapes=[pltpu.VMEM((2 * width, 2 * width), FULL)],
        name="finish",
        cost_estimate=pl.CostEstimate(
            flops=240 * width**3, bytes_accessed=84 * width**2, transcendentals=0
        ),
    )(place, mine, other, *factors)


def swap(value, axis, step):
    size = lax.axis_size(axis)
    return lax.ppermute(value, axis, [(i, i ^ step) for i in range(size)])


def exchange(value, axes):
    return lax.all_to_all(value, axes, 0, 0, tiled=True)


def pieces_of(value, axis):
    return [value] + [swap(value, axis, step) for step in range(1, lax.axis_size(axis))]


def placed(pieces, axis):
    me = lax.axis_index(axis)
    size = pieces[0].shape[0]
    out = jnp.zeros((len(pieces) * size, *pieces[0].shape[1:]), pieces[0].dtype)
    for step, piece in enumerate(pieces):
        out = lax.dynamic_update_slice_in_dim(out, piece, (me ^ step) * size, 0)
    return out


def together(*values):
    return lax.optimization_barrier(values)


def body(
    trail,
    lower_new,
    upper_new,
    lot,
    lower_old,
    uol,
    upper_old,
    ldn,
    udn,
    lin,
    uin,
    ldo,
    udo,
    lio,
    uio,
):
    row, col = ("z", "y"), ("x", "c")
    count = lax.axis_size(col)
    ranks = lax.axis_size(row)

    lower_mine = jnp.concatenate((lower_new.T, lower_old.T), axis=0)
    lower_stack = lax.all_gather(lower_mine, col, axis=0, tiled=True)
    small = prepare(lot, uol, ldn, udn, lin, uin, lio, uio)
    *near, small = together(*pieces_of(upper_new, "z"), *pieces_of(upper_old, "y"), small)
    near_new, near_old = together(placed(near[:4], "z"), placed(near[4:], "y"))
    pieces = pieces_of(near_new, "y") + pieces_of(near_old, "z")
    upper_triple, lower_triple = small[3], small[5]

    band = band_products(lower_triple, lio, lower_stack, trail, ranks, count)
    *pieces, _ = together(*pieces, band)
    band = lax.all_to_all(band, row, 0, 0, tiled=True)

    place = jnp.stack([lax.axis_index(a) for a in row + col]).astype(jnp.int32)
    mine, other, strip = panel_products(
        place, upper_triple, uio, lower_stack, trail, pieces, count
    )
    mine = mine + swap(other, "c", 1)
    mine = mine[0] + sum(swap(mine[k], "x", k) for k in (1, 2, 3))
    mine, band = together(mine, band.sum(0))
    band_right = -lax.all_gather(-band, row, axis=0, tiled=True)
    mine = exchange(mine, row).sum(0)
    mine = exchange(jnp.broadcast_to(mine[None], (ranks, *mine.shape)), row)
    mine = exchange(jnp.broadcast_to(mine[None], (4, *mine.shape)), "x")
    mine, strip = together(mine, strip)
    strip = exchange(strip.reshape(count, -1, strip.shape[1]), col)
    other = swap(mine, "c", 1)
    corner_old, strip_top, band_left = finish(
        place, mine, other, *small, lot, uol, lin, uin, ldo, udo, lio, uio
    )
    strip, corner_old, band_right = together(strip, corner_old, band_right)
    return corner_old, strip_top, strip.sum(0), band_left, band_right


def solution(mesh):
    fine = Mesh(mesh.devices.reshape(4, 4, 4, 2), ("z", "y", "x", "c"))
    row, col = ("z", "y"), ("x", "c")
    split, whole = P(row, col), P()
    return jax.shard_map(
        body,
        mesh=fine,
        in_specs=(split, split, split, whole, split, whole, split) + (whole,) * 8,
        out_specs=(whole, whole, P(row + col, None), whole, P(None, col)),
        check_vma=False,
    )
```

```python
import functools

import jax
import jax.numpy as jnp
from jax import lax
from jax.experimental import pallas as pl
from jax.experimental.pallas import tpu as pltpu
from jax.sharding import Mesh, PartitionSpec as P

HALF = jnp.bfloat16
FULL = jnp.float32
VMEM = pl.BlockSpec(memory_space=pltpu.VMEM)


def mul(left, right, dims):
    return lax.dot_general(left, right, (dims, ((), ())), preferred_element_type=FULL)


def parts(value):
    high = value.astype(HALF)
    return high, (value - high.astype(FULL)).astype(HALF)


def close(left, right, dims=((1,), (0,))):
    (lh, ll), (rh, rl) = left, right
    return mul(lh, rl, dims) + mul(ll, rh, dims) + mul(lh, rh, dims)


def times(left, right):
    return close(parts(left), parts(right))


def far(*arrays):
    return [pltpu.with_memory_space_constraint(a, pltpu.HBM) for a in arrays]


def prepare_kernel(lot, uol, ldn, udn, lin, uin, lio, uio, *out):
    x_new, y_new, upper_pair, upper_triple, lower_pair, lower_triple, side_high, side_low = out
    width = lin.shape[0]
    upper = times(uol[...].T, uio[...].T)
    lower = times(lio[...].T, lot[...].T)
    x_new[...] = times(ldn[...].T, lin[...].T)
    y_new[...] = times(uin[...].T, udn[...].T)
    upper_pair[...] = upper
    lower_pair[...] = lower
    triple = times(uin[...].T, upper)
    upper_triple[...] = triple
    side_high[:width, :], side_low[:width, :] = parts(triple)
    side_high[width:, :], side_low[width:, :] = parts(-uio[...].T)
    lower_triple[...] = times(lower, lin[...].T)


def prepare(*factors):
    width = factors[0].shape[0]
    return pl.pallas_call(
        prepare_kernel,
        out_shape=(jax.ShapeDtypeStruct((width, width), FULL),) * 6
        + (jax.ShapeDtypeStruct((2 * width, width), HALF),) * 2,
        in_specs=[VMEM] * len(factors),
        out_specs=(VMEM,) * 8,
        name="prepare",
        cost_estimate=pl.CostEstimate(
            flops=36 * width**3, bytes_accessed=56 * width**2, transcendentals=0
        ),
    )(*factors)


def lower_rows(lower, panel, count, piece):
    return jnp.concatenate(
        [
            lower[pl.ds((2 * k + panel) * piece, piece), :]
            for k in range(count)
        ],
        axis=0,
    )


def band_kernel(count, triple, lio, lower, trail, out, weights):
    width = lio.shape[0]
    piece = width // count

    @pl.when(pl.program_id(0) == 0)
    def _():
        new = parts(lower_rows(lower, 0, count, piece))
        old = parts(lower_rows(lower, 1, count, piece))
        weight = close(parts(triple[...]), new) - close(parts(lio[...].T), old)
        weights[:width, :], weights[width:, :] = parts(weight)

    high, low = parts(trail[...])
    both = mul(weights[...], high, ((1,), (0,)))
    band = mul(weights[:width, :], low, ((1,), (0,))) + both[width:, :] + both[:width, :]
    size = out.shape[1]
    for k in range(out.shape[0]):
        out[k] = band[k * size : (k + 1) * size, :]


def band_products(triple, lio, lower, trail, ranks, count, tile=512):
    rows, columns = trail.shape
    width = lio.shape[0]
    once = pl.Buffered(1)
    triple, lio, lower, trail = far(triple, lio, lower, trail)
    return pl.pallas_call(
        functools.partial(band_kernel, count),
        out_shape=jax.ShapeDtypeStruct((ranks, width // ranks, columns), FULL),
        grid=(columns // tile,),
        in_specs=[
            pl.BlockSpec((width, width), lambda j: (0, 0), pipeline_mode=once),
            pl.BlockSpec((width, width), lambda j: (0, 0), pipeline_mode=once),
            pl.BlockSpec((2 * width, rows), lambda j: (0, 0), pipeline_mode=once),
            pl.BlockSpec((rows, tile), lambda j: (0, j)),
        ],
        out_specs=pl.BlockSpec((ranks, width // ranks, tile), lambda j: (0, 0, j)),
        scratch_shapes=[pltpu.VMEM((2 * width, rows), HALF)],
        compiler_params=pltpu.CompilerParams(vmem_limit_bytes=24 << 20),
        name="band_products",
        cost_estimate=pl.CostEstimate(
            flops=6 * width * rows * columns,
            bytes_accessed=4 * (rows * columns + 2 * width * rows + width * columns),
            transcendentals=0,
        ),
    )(triple, lio, lower, trail)


def panel_kernel(count, tile, place, side_high, side_low, lower, trail, *rest):
    pieces = rest[:8]
    mine, other, strip, upper_high, upper_low, inner = rest[8:]
    width = side_high.shape[1]
    z, y, x, c = place[0], place[1], place[2], place[3]
    piece = width // count

    def assemble():
        inner[...] = jnp.zeros_like(inner)
        chunk = pieces[0].shape[0] // 4
        for k in range(8):
            for q in range(4):
                rank = 4 * (z ^ (k - 4)) + q if k >= 4 else 4 * q + (y ^ k)
                start = (k // 4) * width + rank * chunk
                at = pl.ds(pl.multiple_of(start, chunk), chunk)
                upper_high[at, :], upper_low[at, :] = parts(
                    pieces[k][q * chunk : (q + 1) * chunk, :]
                )

    def step(lower_tile, trail_tile, strip_tile):
        pl.when(pl.program_id(0) == 0)(assemble)
        product = close(
            parts(trail_tile[...]), (upper_high[...], upper_low[...]), ((1,), (1,))
        )
        product = parts(product)
        strip_tile[...] = close(product, (side_high[...], side_low[...]))
        for panel in range(2):
            left = parts(lower_rows(lower_tile, panel, count, piece))
            inner[panel * width : (panel + 1) * width, :] += close(left, product)

    pltpu.emit_pipeline(
        step,
        grid=(trail.shape[0] // tile,),
        in_specs=[
            pl.BlockSpec((lower.shape[0], tile), lambda i: (0, i)),
            pl.BlockSpec((tile, trail.shape[1]), lambda i: (i, 0)),
        ],
        out_specs=[pl.BlockSpec((tile, width), lambda i: (i, 0))],
    )(lower, trail, strip)

    rows, share = mine.shape[2], width // 4
    for k in range(4):
        for p in range(mine.shape[1]):
            start, column = (x ^ k) * share + rows * (p // 2), width * (p % 2)
            near = pl.ds(pl.multiple_of(c * width + start, rows), rows)
            beside = pl.ds(pl.multiple_of((1 - c) * width + start, rows), rows)
            mine[k, p] = inner[near, column : column + width]
            other[k, p] = inner[beside, column : column + width]


def panel_products(place, sides, lower, trail, pieces, count, tile=256):
    rows, columns = trail.shape
    width = sides[0].shape[1]
    share = (4, 16, width // 32, width)
    *sides, lower, trail = far(*sides, lower, trail)
    hbm = pl.BlockSpec(memory_space=pltpu.HBM)
    return pl.pallas_call(
        functools.partial(panel_kernel, count, tile),
        out_shape=(
            jax.ShapeDtypeStruct(share, FULL),
            jax.ShapeDtypeStruct(share, FULL),
            jax.ShapeDtypeStruct((rows, width), FULL),
        ),
        in_specs=[pl.BlockSpec(memory_space=pltpu.SMEM)] + [VMEM] * 2 + [hbm] * 2 + [VMEM] * 8,
        out_specs=(VMEM, VMEM, hbm),
        scratch_shapes=[pltpu.VMEM((2 * width, columns), HALF)] * 2
        + [pltpu.VMEM((2 * width, 2 * width), FULL)],
        compiler_params=pltpu.CompilerParams(vmem_limit_bytes=36 << 20),
        name="panel_products",
        cost_estimate=pl.CostEstimate(
            flops=3 * (4 * width * rows * columns + 12 * width * width * rows),
            bytes_accessed=4 * (rows * columns + 2 * width * columns + 4 * width * rows),
            transcendentals=0,
        ),
    )(place, *sides, lower, trail, *pieces)


def finish_kernel(
    place,
    mine,
    other,
    x_new,
    y_new,
    upper_pair,
    upper_triple,
    lower_pair,
    lower_triple,
    lot,
    uol,
    lin,
    uin,
    ldo,
    udo,
    lio,
    uio,
    corner_out,
    top_out,
    left_out,
    inner,
):
    width = lin.shape[0]
    c = place[3]
    rows, share = mine.shape[1], width // 4
    for k in range(4):
        for p in range(mine.shape[0] // 4):
            start, column = k * share + rows * (p // 2), width * (p % 2)
            near = pl.ds(pl.multiple_of(c * width + start, rows), rows)
            beside = pl.ds(pl.multiple_of((1 - c) * width + start, rows), rows)
            inner[near, column : column + width] = mine[4 * p + k]
            inner[beside, column : column + width] = other[4 * p + k]
    row = lax.broadcasted_iota(jnp.int32, (width, width), 0)
    column = lax.broadcasted_iota(jnp.int32, (width, width), 1)
    below = row > column
    g11, g12 = inner[:width, :width], inner[:width, width:]
    g21, g22 = inner[width:, :width], inner[width:, width:]
    lin_t, uin_t, lio_t, uio_t = lin[...].T, uin[...].T, lio[...].T, uio[...].T
    inside = jnp.where(below, times(x_new[...], g11), times(g11, y_new[...]))
    corner = times(times(lin_t, inside), uin_t)
    top = times(times(lin_t, g12), uio_t) - times(corner, upper_pair[...])
    left = times(lio_t, times(g21, uin_t)) - times(lower_pair[...], corner)
    top_out[...] = top
    left_out[...] = left
    outer = times(lower_triple[...], g12) - times(lio_t, g22)
    under = times(g21, upper_triple[...]) - times(g22, uio_t)
    lower_grad = -(times(left, uol[...].T) + outer)
    upper_grad = -(times(lot[...].T, top) + under)
    inside = jnp.where(
        below, times(ldo[...].T, lower_grad), times(upper_grad, udo[...].T)
    )
    corner_out[...] = times(times(lio_t, inside), uio_t)


def finish(place, mine, other, *factors):
    width = factors[0].shape[0]
    mine, other = (pltpu.with_memory_space_constraint(a, pltpu.VMEM) for a in (mine, other))
    return pl.pallas_call(
        finish_kernel,
        out_shape=(jax.ShapeDtypeStruct((width, width), FULL),) * 3,
        in_specs=[pl.BlockSpec(memory_space=pltpu.SMEM)] + [VMEM] * (2 + len(factors)),
        out_specs=(VMEM,) * 3,
        scratch_shapes=[pltpu.VMEM((2 * width, 2 * width), FULL)],
        name="finish",
        cost_estimate=pl.CostEstimate(
            flops=240 * width**3, bytes_accessed=84 * width**2, transcendentals=0
        ),
    )(place, mine, other, *factors)


def swap(value, axis, step):
    size = lax.axis_size(axis)
    return lax.ppermute(value, axis, [(i, i ^ step) for i in range(size)])


def exchange(value, axes):
    return lax.all_to_all(value, axes, 0, 0, tiled=True)


def pieces_of(value, axis):
    return [value] + [swap(value, axis, step) for step in range(1, lax.axis_size(axis))]


def placed(pieces, axis):
    me = lax.axis_index(axis)
    size = pieces[0].shape[0]
    out = jnp.zeros((len(pieces) * size, *pieces[0].shape[1:]), pieces[0].dtype)
    for step, piece in enumerate(pieces):
        out = lax.dynamic_update_slice_in_dim(out, piece, (me ^ step) * size, 0)
    return out


def together(*values):
    return lax.optimization_barrier(values)


def body(
    trail,
    lower_new,
    upper_new,
    lot,
    lower_old,
    uol,
    upper_old,
    ldn,
    udn,
    lin,
    uin,
    ldo,
    udo,
    lio,
    uio,
):
    row, col = ("z", "y"), ("x", "c")
    count = lax.axis_size(col)
    ranks = lax.axis_size(row)

    lower_mine = jnp.concatenate((lower_new.T, lower_old.T), axis=0)
    lower_stack = lax.all_gather(lower_mine, col, axis=0, tiled=True)
    small = prepare(lot, uol, ldn, udn, lin, uin, lio, uio)
    *near, small = together(*pieces_of(upper_new, "z"), *pieces_of(upper_old, "y"), small)
    near_new, near_old = together(placed(near[:4], "z"), placed(near[4:], "y"))
    pieces = pieces_of(near_new, "y") + pieces_of(near_old, "z")
    *small, side_high, side_low = small

    band = band_products(small[5], lio, lower_stack, trail, ranks, count)
    *pieces, _ = together(*pieces, band)
    band = lax.all_to_all(band, row, 0, 0, tiled=True)

    place = jnp.stack([lax.axis_index(a) for a in row + col]).astype(jnp.int32)
    mine, other, strip = panel_products(
        place, (side_high, side_low), lower_stack, trail, pieces, count
    )
    mine = mine + swap(other, "c", 1)
    mine = mine[0] + sum(swap(mine[k], "x", k) for k in (1, 2, 3))
    mine, band = together(mine, band.sum(0))
    band_right = -lax.all_gather(-band, row, axis=0, tiled=True)
    mine = exchange(mine, row).sum(0)
    mine = exchange(jnp.broadcast_to(mine[None], (4 * ranks, *mine.shape)), row + ("x",))
    mine, strip = together(mine, strip)
    strip = exchange(strip.reshape(count, -1, strip.shape[1]), col)
    other = swap(mine, "c", 1)
    corner_old, strip_top, band_left = finish(
        place, mine, other, *small, lot, uol, lin, uin, ldo, udo, lio, uio
    )
    strip, corner_old, band_right = together(strip, corner_old, band_right)
    return corner_old, strip_top, strip.sum(0), band_left, band_right


def solution(mesh):
    fine = Mesh(mesh.devices.reshape(4, 4, 4, 2), ("z", "y", "x", "c"))
    row, col = ("z", "y"), ("x", "c")
    split, whole = P(row, col), P()
    return jax.shard_map(
        body,
        mesh=fine,
        in_specs=(split, split, split, whole, split, whole, split) + (whole,) * 8,
        out_specs=(whole, whole, P(row + col, None), whole, P(None, col)),
        check_vma=False,
    )
```

```python
import functools

import jax
import jax.numpy as jnp
from jax import lax
from jax.experimental import pallas as pl
from jax.experimental.pallas import tpu as pltpu
from jax.sharding import Mesh, PartitionSpec as P

HALF = jnp.bfloat16
FULL = jnp.float32
VMEM = pl.BlockSpec(memory_space=pltpu.VMEM)


def mul(left, right, dims):
    return lax.dot_general(left, right, (dims, ((), ())), preferred_element_type=FULL)


def parts(value):
    high = value.astype(HALF)
    return high, (value - high.astype(FULL)).astype(HALF)


def close(left, right, dims=((1,), (0,))):
    (lh, ll), (rh, rl) = left, right
    return mul(lh, rl, dims) + mul(ll, rh, dims) + mul(lh, rh, dims)


def times(left, right):
    return close(parts(left), parts(right))


def far(*arrays):
    return [pltpu.with_memory_space_constraint(a, pltpu.HBM) for a in arrays]


def prepare_kernel(lot, uol, ldn, udn, lin, uin, lio, uio, *out):
    x_new, y_new, upper_pair, upper_triple, lower_pair, lower_triple, side_high, side_low = out
    width = lin.shape[0]
    upper = times(uol[...].T, uio[...].T)
    lower = times(lio[...].T, lot[...].T)
    x_new[...] = times(ldn[...].T, lin[...].T)
    y_new[...] = times(uin[...].T, udn[...].T)
    upper_pair[...] = upper
    lower_pair[...] = lower
    triple = times(uin[...].T, upper)
    upper_triple[...] = triple
    side_high[:width, :], side_low[:width, :] = parts(triple)
    side_high[width:, :], side_low[width:, :] = parts(-uio[...].T)
    lower_triple[...] = times(lower, lin[...].T)


def prepare(*factors):
    width = factors[0].shape[0]
    return pl.pallas_call(
        prepare_kernel,
        out_shape=(jax.ShapeDtypeStruct((width, width), FULL),) * 6
        + (jax.ShapeDtypeStruct((2 * width, width), HALF),) * 2,
        in_specs=[VMEM] * len(factors),
        out_specs=(VMEM,) * 8,
        name="prepare",
        cost_estimate=pl.CostEstimate(
            flops=36 * width**3, bytes_accessed=56 * width**2, transcendentals=0
        ),
    )(*factors)


def lower_rows(lower, panel, count, piece):
    return jnp.concatenate(
        [
            lower[pl.ds((2 * k + panel) * piece, piece), :]
            for k in range(count)
        ],
        axis=0,
    )


def band_kernel(count, triple, lio, lower, trail, out, weights):
    width = lio.shape[0]
    piece = width // count

    @pl.when(pl.program_id(0) == 0)
    def _():
        new = parts(lower_rows(lower, 0, count, piece))
        old = parts(lower_rows(lower, 1, count, piece))
        weight = close(parts(lio[...].T), old) - close(parts(triple[...]), new)
        weights[:width, :], weights[width:, :] = parts(weight)

    high, low = parts(trail[...])
    both = mul(weights[...], high, ((1,), (0,)))
    band = mul(weights[:width, :], low, ((1,), (0,))) + both[width:, :] + both[:width, :]
    size = out.shape[1]
    for k in range(out.shape[0]):
        out[k] = band[k * size : (k + 1) * size, :]


def band_products(triple, lio, lower, trail, ranks, count, tile=1024):
    rows, columns = trail.shape
    width = lio.shape[0]
    once = pl.Buffered(1)
    triple, lio, lower, trail = far(triple, lio, lower, trail)
    return pl.pallas_call(
        functools.partial(band_kernel, count),
        out_shape=jax.ShapeDtypeStruct((ranks, width // ranks, columns), FULL),
        grid=(columns // tile,),
        in_specs=[
            pl.BlockSpec((width, width), lambda j: (0, 0), pipeline_mode=once),
            pl.BlockSpec((width, width), lambda j: (0, 0), pipeline_mode=once),
            pl.BlockSpec((2 * width, rows), lambda j: (0, 0), pipeline_mode=once),
            pl.BlockSpec((rows, tile), lambda j: (0, j)),
        ],
        out_specs=pl.BlockSpec((ranks, width // ranks, tile), lambda j: (0, 0, j)),
        scratch_shapes=[pltpu.VMEM((2 * width, rows), HALF)],
        compiler_params=pltpu.CompilerParams(vmem_limit_bytes=24 << 20),
        name="band_products",
        cost_estimate=pl.CostEstimate(
            flops=6 * width * rows * columns,
            bytes_accessed=4 * (rows * columns + 2 * width * rows + width * columns),
            transcendentals=0,
        ),
    )(triple, lio, lower, trail)


def panel_kernel(count, tile, place, side_high, side_low, lower, trail, *rest):
    pieces = rest[:8]
    mine, other, strip, upper_high, upper_low, inner = rest[8:]
    width = side_high.shape[1]
    z, y, x, c = place[0], place[1], place[2], place[3]
    piece = width // count

    def assemble():
        inner[...] = jnp.zeros_like(inner)
        chunk = pieces[0].shape[0] // 4
        for k in range(8):
            for q in range(4):
                rank = 4 * (z ^ (k - 4)) + q if k >= 4 else 4 * q + (y ^ k)
                start = (k // 4) * width + rank * chunk
                at = pl.ds(pl.multiple_of(start, chunk), chunk)
                upper_high[at, :], upper_low[at, :] = parts(
                    pieces[k][q * chunk : (q + 1) * chunk, :]
                )

    def step(lower_tile, trail_tile, strip_tile):
        pl.when(pl.program_id(0) == 0)(assemble)
        product = close(
            parts(trail_tile[...]), (upper_high[...], upper_low[...]), ((1,), (1,))
        )
        product = parts(product)
        strip_tile[...] = close(product, (side_high[...], side_low[...]))
        for panel in range(2):
            left = parts(lower_rows(lower_tile, panel, count, piece))
            inner[panel * width : (panel + 1) * width, :] += close(left, product)

    pltpu.emit_pipeline(
        step,
        grid=(trail.shape[0] // tile,),
        in_specs=[
            pl.BlockSpec((lower.shape[0], tile), lambda i: (0, i)),
            pl.BlockSpec((tile, trail.shape[1]), lambda i: (i, 0)),
        ],
        out_specs=[pl.BlockSpec((tile, width), lambda i: (i, 0))],
    )(lower, trail, strip)

    rows, share = mine.shape[2], width // 4
    for k in range(4):
        for p in range(mine.shape[1]):
            start, column = (x ^ k) * share + rows * (p // 2), width * (p % 2)
            near = pl.ds(pl.multiple_of(c * width + start, rows), rows)
            beside = pl.ds(pl.multiple_of((1 - c) * width + start, rows), rows)
            mine[k, p] = inner[near, column : column + width]
            other[k, p] = inner[beside, column : column + width]


def panel_products(place, sides, lower, trail, pieces, count, tile=256):
    rows, columns = trail.shape
    width = sides[0].shape[1]
    share = (4, 16, width // 32, width)
    *sides, lower, trail = far(*sides, lower, trail)
    hbm = pl.BlockSpec(memory_space=pltpu.HBM)
    return pl.pallas_call(
        functools.partial(panel_kernel, count, tile),
        out_shape=(
            jax.ShapeDtypeStruct(share, FULL),
            jax.ShapeDtypeStruct(share, FULL),
            jax.ShapeDtypeStruct((rows, width), FULL),
        ),
        in_specs=[pl.BlockSpec(memory_space=pltpu.SMEM)] + [VMEM] * 2 + [hbm] * 2 + [VMEM] * 8,
        out_specs=(VMEM, VMEM, hbm),
        scratch_shapes=[pltpu.VMEM((2 * width, columns), HALF)] * 2
        + [pltpu.VMEM((2 * width, 2 * width), FULL)],
        compiler_params=pltpu.CompilerParams(vmem_limit_bytes=36 << 20),
        name="panel_products",
        cost_estimate=pl.CostEstimate(
            flops=3 * (4 * width * rows * columns + 12 * width * width * rows),
            bytes_accessed=4 * (rows * columns + 2 * width * columns + 4 * width * rows),
            transcendentals=0,
        ),
    )(place, *sides, lower, trail, *pieces)


def finish_kernel(
    place,
    mine,
    other,
    x_new,
    y_new,
    upper_pair,
    upper_triple,
    lower_pair,
    lower_triple,
    lot,
    uol,
    lin,
    uin,
    ldo,
    udo,
    lio,
    uio,
    corner_out,
    top_out,
    left_out,
    inner,
):
    width = lin.shape[0]
    c = place[3]
    rows, share = mine.shape[1], width // 4
    for k in range(4):
        for p in range(mine.shape[0] // 4):
            start, column = k * share + rows * (p // 2), width * (p % 2)
            near = pl.ds(pl.multiple_of(c * width + start, rows), rows)
            beside = pl.ds(pl.multiple_of((1 - c) * width + start, rows), rows)
            inner[near, column : column + width] = mine[4 * p + k]
            inner[beside, column : column + width] = other[4 * p + k]
    row = lax.broadcasted_iota(jnp.int32, (width, width), 0)
    column = lax.broadcasted_iota(jnp.int32, (width, width), 1)
    below = row > column
    g11, g12 = inner[:width, :width], inner[:width, width:]
    g21, g22 = inner[width:, :width], inner[width:, width:]
    lin_t, uin_t, lio_t, uio_t = lin[...].T, uin[...].T, lio[...].T, uio[...].T
    inside = jnp.where(below, times(x_new[...], g11), times(g11, y_new[...]))
    corner = times(times(lin_t, inside), uin_t)
    top = times(times(lin_t, g12), uio_t) - times(corner, upper_pair[...])
    left = times(lio_t, times(g21, uin_t)) - times(lower_pair[...], corner)
    top_out[...] = top
    left_out[...] = left
    outer = times(lower_triple[...], g12) - times(lio_t, g22)
    under = times(g21, upper_triple[...]) - times(g22, uio_t)
    lower_grad = -(times(left, uol[...].T) + outer)
    upper_grad = -(times(lot[...].T, top) + under)
    inside = jnp.where(
        below, times(ldo[...].T, lower_grad), times(upper_grad, udo[...].T)
    )
    corner_out[...] = times(times(lio_t, inside), uio_t)


def finish(place, mine, other, *factors):
    width = factors[0].shape[0]
    mine, other = (pltpu.with_memory_space_constraint(a, pltpu.VMEM) for a in (mine, other))
    return pl.pallas_call(
        finish_kernel,
        out_shape=(jax.ShapeDtypeStruct((width, width), FULL),) * 3,
        in_specs=[pl.BlockSpec(memory_space=pltpu.SMEM)] + [VMEM] * (2 + len(factors)),
        out_specs=(VMEM,) * 3,
        scratch_shapes=[pltpu.VMEM((2 * width, 2 * width), FULL)],
        name="finish",
        cost_estimate=pl.CostEstimate(
            flops=240 * width**3, bytes_accessed=84 * width**2, transcendentals=0
        ),
    )(place, mine, other, *factors)


def swap(value, axis, step):
    size = lax.axis_size(axis)
    return lax.ppermute(value, axis, [(i, i ^ step) for i in range(size)])


def exchange(value, axes):
    return lax.all_to_all(value, axes, 0, 0, tiled=True)


def pieces_of(value, axis):
    return [value] + [swap(value, axis, step) for step in range(1, lax.axis_size(axis))]


def placed(pieces, axis):
    me = lax.axis_index(axis)
    size = pieces[0].shape[0]
    out = jnp.zeros((len(pieces) * size, *pieces[0].shape[1:]), pieces[0].dtype)
    for step, piece in enumerate(pieces):
        out = lax.dynamic_update_slice_in_dim(out, piece, (me ^ step) * size, 0)
    return out


def together(*values):
    return lax.optimization_barrier(values)


def body(
    trail,
    lower_new,
    upper_new,
    lot,
    lower_old,
    uol,
    upper_old,
    ldn,
    udn,
    lin,
    uin,
    ldo,
    udo,
    lio,
    uio,
):
    row, col = ("z", "y"), ("x", "c")
    count = lax.axis_size(col)
    ranks = lax.axis_size(row)

    lower_mine = jnp.concatenate((lower_new.T, lower_old.T), axis=0)
    lower_stack = lax.all_gather(lower_mine, col, axis=0, tiled=True)
    small = prepare(lot, uol, ldn, udn, lin, uin, lio, uio)
    *near, small = together(*pieces_of(upper_new, "z"), *pieces_of(upper_old, "y"), small)
    near_new, near_old = together(placed(near[:4], "z"), placed(near[4:], "y"))
    pieces = pieces_of(near_new, "y") + pieces_of(near_old, "z")
    *small, side_high, side_low = small

    band = band_products(small[5], lio, lower_stack, trail, ranks, count)
    *pieces, _ = together(*pieces, band)
    band = lax.all_to_all(band, row, 0, 0, tiled=True)

    place = jnp.stack([lax.axis_index(a) for a in row + col]).astype(jnp.int32)
    mine, other, strip = panel_products(
        place, (side_high, side_low), lower_stack, trail, pieces, count
    )
    mine = mine + swap(other, "c", 1)
    mine = mine[0] + sum(swap(mine[k], "x", k) for k in (1, 2, 3))
    mine, band = together(mine, band.sum(0))
    band = lax.all_gather(band, row, axis=0, tiled=True)
    mine = exchange(mine, row).sum(0)
    mine = exchange(jnp.broadcast_to(mine[None], (4 * ranks, *mine.shape)), row + ("x",))
    mine, strip = together(mine, strip)
    strip = exchange(strip.reshape(count, -1, strip.shape[1]), col)
    other = swap(mine, "c", 1)
    corner_old, strip_top, band_left = finish(
        place, mine, other, *small, lot, uol, lin, uin, ldo, udo, lio, uio
    )
    band, strip_bottom = together(band, strip.sum(0))
    return corner_old, strip_top, strip_bottom, band_left, -band


def solution(mesh):
    fine = Mesh(mesh.devices.reshape(4, 4, 4, 2), ("z", "y", "x", "c"))
    row, col = ("z", "y"), ("x", "c")
    split, whole = P(row, col), P()
    return jax.shard_map(
        body,
        mesh=fine,
        in_specs=(split, split, split, whole, split, whole, split) + (whole,) * 8,
        out_specs=(whole, whole, P(row + col, None), whole, P(None, col)),
        check_vma=False,
    )
```

```python
import functools

import jax
import jax.numpy as jnp
from jax import lax
from jax.experimental import pallas as pl
from jax.experimental.pallas import tpu as pltpu
from jax.sharding import Mesh, PartitionSpec as P

HALF = jnp.bfloat16
FULL = jnp.float32
VMEM = pl.BlockSpec(memory_space=pltpu.VMEM)


def mul(left, right, dims):
    return lax.dot_general(left, right, (dims, ((), ())), preferred_element_type=FULL)


def parts(value):
    high = value.astype(HALF)
    return high, (value - high.astype(FULL)).astype(HALF)


def close(left, right, dims=((1,), (0,))):
    (lh, ll), (rh, rl) = left, right
    return mul(lh, rl, dims) + mul(ll, rh, dims) + mul(lh, rh, dims)


def times(left, right):
    return close(parts(left), parts(right))


def far(*arrays):
    return [pltpu.with_memory_space_constraint(a, pltpu.HBM) for a in arrays]


def prepare_kernel(lot, uol, ldn, udn, lin, uin, lio, uio, *out):
    x_new, y_new, upper_pair, upper_triple, lower_pair, lower_triple, side_high, side_low = out
    width = lin.shape[0]
    upper = times(uol[...].T, uio[...].T)
    lower = times(lio[...].T, lot[...].T)
    x_new[...] = times(ldn[...].T, lin[...].T)
    y_new[...] = times(uin[...].T, udn[...].T)
    upper_pair[...] = upper
    lower_pair[...] = lower
    triple = times(uin[...].T, upper)
    upper_triple[...] = triple
    side_high[:width, :], side_low[:width, :] = parts(triple)
    side_high[width:, :], side_low[width:, :] = parts(-uio[...].T)
    lower_triple[...] = times(lower, lin[...].T)


def prepare(*factors):
    width = factors[0].shape[0]
    return pl.pallas_call(
        prepare_kernel,
        out_shape=(jax.ShapeDtypeStruct((width, width), FULL),) * 6
        + (jax.ShapeDtypeStruct((2 * width, width), HALF),) * 2,
        in_specs=[VMEM] * len(factors),
        out_specs=(VMEM,) * 8,
        name="prepare",
        cost_estimate=pl.CostEstimate(
            flops=36 * width**3, bytes_accessed=56 * width**2, transcendentals=0
        ),
    )(*factors)


def lower_rows(lower, panel, count, piece):
    return jnp.concatenate(
        [
            lower[pl.ds((2 * k + panel) * piece, piece), :]
            for k in range(count)
        ],
        axis=0,
    )


def band_kernel(count, triple, lio, lower, trail, out, weights):
    width = lio.shape[0]
    piece = width // count

    @pl.when(pl.program_id(0) == 0)
    def _():
        new = parts(lower_rows(lower, 0, count, piece))
        old = parts(lower_rows(lower, 1, count, piece))
        weight = close(parts(triple[...]), new) - close(parts(lio[...].T), old)
        weights[:width, :], weights[width:, :] = parts(weight)

    high, low = parts(trail[...])
    both = mul(weights[...], high, ((1,), (0,)))
    band = mul(weights[:width, :], low, ((1,), (0,))) + both[width:, :] + both[:width, :]
    size = out.shape[1]
    for k in range(out.shape[0]):
        out[k] = band[k * size : (k + 1) * size, :]


def band_products(triple, lio, lower, trail, ranks, count, tile=1024):
    rows, columns = trail.shape
    width = lio.shape[0]
    once = pl.Buffered(1)
    triple, lio, lower, trail = far(triple, lio, lower, trail)
    return pl.pallas_call(
        functools.partial(band_kernel, count),
        out_shape=jax.ShapeDtypeStruct((ranks, width // ranks, columns), FULL),
        grid=(columns // tile,),
        in_specs=[
            pl.BlockSpec((width, width), lambda j: (0, 0), pipeline_mode=once),
            pl.BlockSpec((width, width), lambda j: (0, 0), pipeline_mode=once),
            pl.BlockSpec((2 * width, rows), lambda j: (0, 0), pipeline_mode=once),
            pl.BlockSpec((rows, tile), lambda j: (0, j)),
        ],
        out_specs=pl.BlockSpec((ranks, width // ranks, tile), lambda j: (0, 0, j)),
        scratch_shapes=[pltpu.VMEM((2 * width, rows), HALF)],
        compiler_params=pltpu.CompilerParams(vmem_limit_bytes=24 << 20),
        name="band_products",
        cost_estimate=pl.CostEstimate(
            flops=6 * width * rows * columns,
            bytes_accessed=4 * (rows * columns + 2 * width * rows + width * columns),
            transcendentals=0,
        ),
    )(triple, lio, lower, trail)


def panel_kernel(count, tile, place, side_high, side_low, lower, trail, *rest):
    pieces = rest[:8]
    mine, other, strip, strip_beside, upper_high, upper_low, inner = rest[8:]
    width = side_high.shape[1]
    z, y, x, c = place[0], place[1], place[2], place[3]
    piece = width // count

    def assemble():
        inner[...] = jnp.zeros_like(inner)
        chunk = pieces[0].shape[0] // 4
        for k in range(8):
            for q in range(4):
                rank = 4 * (z ^ (k - 4)) + q if k >= 4 else 4 * q + (y ^ k)
                start = (k // 4) * width + rank * chunk
                at = pl.ds(pl.multiple_of(start, chunk), chunk)
                upper_high[at, :], upper_low[at, :] = parts(
                    pieces[k][q * chunk : (q + 1) * chunk, :]
                )

    def step(lower_tile, trail_tile, near_tile, beside_tile):
        pl.when(pl.program_id(0) == 0)(assemble)
        product = close(
            parts(trail_tile[...]), (upper_high[...], upper_low[...]), ((1,), (1,))
        )
        product = parts(product)
        result = close(product, (side_high[...], side_low[...]))
        first, second = result[: tile // 2, :], result[tile // 2 :, :]
        near_tile[...] = jnp.where(c == 0, first, second)
        beside_tile[...] = jnp.where(c == 0, second, first)
        for panel in range(2):
            left = parts(lower_rows(lower_tile, panel, count, piece))
            inner[panel * width : (panel + 1) * width, :] += close(left, product)

    pltpu.emit_pipeline(
        step,
        grid=(trail.shape[0] // tile,),
        in_specs=[
            pl.BlockSpec((lower.shape[0], tile), lambda i: (0, i)),
            pl.BlockSpec((tile, trail.shape[1]), lambda i: (i, 0)),
        ],
        out_specs=[pl.BlockSpec((tile // 2, width), lambda i: (i ^ x, 0))] * 2,
    )(lower, trail, strip, strip_beside)

    rows, share = mine.shape[2], width // 4
    for k in range(4):
        for p in range(mine.shape[1]):
            start, column = (x ^ k) * share + rows * (p // 2), width * (p % 2)
            near = pl.ds(pl.multiple_of(c * width + start, rows), rows)
            beside = pl.ds(pl.multiple_of((1 - c) * width + start, rows), rows)
            mine[k, p] = inner[near, column : column + width]
            other[k, p] = inner[beside, column : column + width]


def panel_products(place, sides, lower, trail, pieces, count, tile=256):
    rows, columns = trail.shape
    width = sides[0].shape[1]
    share = (4, 16, width // 32, width)
    *sides, lower, trail = far(*sides, lower, trail)
    hbm = pl.BlockSpec(memory_space=pltpu.HBM)
    return pl.pallas_call(
        functools.partial(panel_kernel, count, tile),
        out_shape=(
            jax.ShapeDtypeStruct(share, FULL),
            jax.ShapeDtypeStruct(share, FULL),
            jax.ShapeDtypeStruct((rows // 2, width), FULL),
            jax.ShapeDtypeStruct((rows // 2, width), FULL),
        ),
        in_specs=[pl.BlockSpec(memory_space=pltpu.SMEM)] + [VMEM] * 2 + [hbm] * 2 + [VMEM] * 8,
        out_specs=(VMEM, VMEM, hbm, hbm),
        scratch_shapes=[pltpu.VMEM((2 * width, columns), HALF)] * 2
        + [pltpu.VMEM((2 * width, 2 * width), FULL)],
        compiler_params=pltpu.CompilerParams(vmem_limit_bytes=36 << 20),
        name="panel_products",
        cost_estimate=pl.CostEstimate(
            flops=3 * (4 * width * rows * columns + 12 * width * width * rows),
            bytes_accessed=4 * (rows * columns + 2 * width * columns + 4 * width * rows),
            transcendentals=0,
        ),
    )(place, *sides, lower, trail, *pieces)


def finish_kernel(
    place,
    mine,
    other,
    x_new,
    y_new,
    upper_pair,
    upper_triple,
    lower_pair,
    lower_triple,
    lot,
    uol,
    lin,
    uin,
    ldo,
    udo,
    lio,
    uio,
    corner_out,
    top_out,
    left_out,
    inner,
):
    width = lin.shape[0]
    c = place[3]
    rows, share = mine.shape[1], width // 4
    for k in range(4):
        for p in range(mine.shape[0] // 4):
            start, column = k * share + rows * (p // 2), width * (p % 2)
            near = pl.ds(pl.multiple_of(c * width + start, rows), rows)
            beside = pl.ds(pl.multiple_of((1 - c) * width + start, rows), rows)
            inner[near, column : column + width] = mine[4 * p + k]
            inner[beside, column : column + width] = other[4 * p + k]
    row = lax.broadcasted_iota(jnp.int32, (width, width), 0)
    column = lax.broadcasted_iota(jnp.int32, (width, width), 1)
    below = row > column
    g11, g12 = inner[:width, :width], inner[:width, width:]
    g21, g22 = inner[width:, :width], inner[width:, width:]
    lin_t, uin_t, lio_t, uio_t = lin[...].T, uin[...].T, lio[...].T, uio[...].T
    inside = jnp.where(below, times(x_new[...], g11), times(g11, y_new[...]))
    corner = times(times(lin_t, inside), uin_t)
    top = times(times(lin_t, g12), uio_t) - times(corner, upper_pair[...])
    left = times(lio_t, times(g21, uin_t)) - times(lower_pair[...], corner)
    top_out[...] = top
    left_out[...] = left
    outer = times(lower_triple[...], g12) - times(lio_t, g22)
    under = times(g21, upper_triple[...]) - times(g22, uio_t)
    lower_grad = -(times(left, uol[...].T) + outer)
    upper_grad = -(times(lot[...].T, top) + under)
    inside = jnp.where(
        below, times(ldo[...].T, lower_grad), times(upper_grad, udo[...].T)
    )
    corner_out[...] = times(times(lio_t, inside), uio_t)


def finish(place, mine, other, *factors):
    width = factors[0].shape[0]
    mine, other = (pltpu.with_memory_space_constraint(a, pltpu.VMEM) for a in (mine, other))
    return pl.pallas_call(
        finish_kernel,
        out_shape=(jax.ShapeDtypeStruct((width, width), FULL),) * 3,
        in_specs=[pl.BlockSpec(memory_space=pltpu.SMEM)] + [VMEM] * (2 + len(factors)),
        out_specs=(VMEM,) * 3,
        scratch_shapes=[pltpu.VMEM((2 * width, 2 * width), FULL)],
        name="finish",
        cost_estimate=pl.CostEstimate(
            flops=240 * width**3, bytes_accessed=84 * width**2, transcendentals=0
        ),
    )(place, mine, other, *factors)


def swap(value, axis, step):
    size = lax.axis_size(axis)
    return lax.ppermute(value, axis, [(i, i ^ step) for i in range(size)])


def exchange(value, axes):
    return lax.all_to_all(value, axes, 0, 0, tiled=True)


def pieces_of(value, axis):
    return [value] + [swap(value, axis, step) for step in range(1, lax.axis_size(axis))]


def placed(pieces, axis):
    me = lax.axis_index(axis)
    size = pieces[0].shape[0]
    out = jnp.zeros((len(pieces) * size, *pieces[0].shape[1:]), pieces[0].dtype)
    for step, piece in enumerate(pieces):
        out = lax.dynamic_update_slice_in_dim(out, piece, (me ^ step) * size, 0)
    return out


def together(*values):
    return lax.optimization_barrier(values)


def body(
    trail,
    lower_new,
    upper_new,
    lot,
    lower_old,
    uol,
    upper_old,
    ldn,
    udn,
    lin,
    uin,
    ldo,
    udo,
    lio,
    uio,
):
    row, col = ("z", "y"), ("x", "c")
    count = lax.axis_size(col)
    ranks = lax.axis_size(row)

    lower_mine = jnp.concatenate((lower_new.T, lower_old.T), axis=0)
    lower_stack = lax.all_gather(lower_mine, col, axis=0, tiled=True)
    small = prepare(lot, uol, ldn, udn, lin, uin, lio, uio)
    *near, small = together(*pieces_of(upper_new, "z"), *pieces_of(upper_old, "y"), small)
    near_new, near_old = together(placed(near[:4], "z"), placed(near[4:], "y"))
    pieces = pieces_of(near_new, "y") + pieces_of(near_old, "z")
    *small, side_high, side_low = small

    band = band_products(small[5], lio, lower_stack, trail, ranks, count)
    *pieces, _ = together(*pieces, band)
    band = lax.all_to_all(band, row, 0, 0, tiled=True)

    place = jnp.stack([lax.axis_index(a) for a in row + col]).astype(jnp.int32)
    mine, other, strip, beside = panel_products(
        place, (side_high, side_low), lower_stack, trail, pieces, count
    )
    mine = mine + swap(other, "c", 1)
    mine = mine[0] + sum(swap(mine[k], "x", k) for k in (1, 2, 3))
    mine, band = together(mine, band.sum(0))
    band_right = -lax.all_gather(-band, row, axis=0, tiled=True)
    beside = swap(beside, "c", 1)
    mine = exchange(mine, row).sum(0)
    mine, beside = together(mine, beside)
    strip = (strip + beside).reshape(4, -1, strip.shape[1])
    arrived = [swap(strip[k], "x", k) for k in (1, 2, 3)]
    mine = exchange(jnp.broadcast_to(mine[None], (4 * ranks, *mine.shape)), row + ("x",))
    mine, *arrived = together(mine, *arrived)
    strip_bottom = strip[0] + sum(arrived)
    other = swap(mine, "c", 1)
    corner_old, strip_top, band_left = finish(
        place, mine, other, *small, lot, uol, lin, uin, ldo, udo, lio, uio
    )
    return corner_old, strip_top, strip_bottom, band_left, band_right


def solution(mesh):
    fine = Mesh(mesh.devices.reshape(4, 4, 4, 2), ("z", "y", "x", "c"))
    row, col = ("z", "y"), ("x", "c")
    split, whole = P(row, col), P()
    return jax.shard_map(
        body,
        mesh=fine,
        in_specs=(split, split, split, whole, split, whole, split) + (whole,) * 8,
        out_specs=(whole, whole, P(row + col, None), whole, P(None, col)),
        check_vma=False,
    )
```

```python
import functools

import jax
import jax.numpy as jnp
from jax import lax
from jax.experimental import pallas as pl
from jax.experimental.pallas import tpu as pltpu
from jax.sharding import Mesh, PartitionSpec as P

HALF = jnp.bfloat16
FULL = jnp.float32
VMEM = pl.BlockSpec(memory_space=pltpu.VMEM)


def mul(left, right, dims):
    return lax.dot_general(left, right, (dims, ((), ())), preferred_element_type=FULL)


def parts(value):
    high = value.astype(HALF)
    return high, (value - high.astype(FULL)).astype(HALF)


def close(left, right, dims=((1,), (0,))):
    (lh, ll), (rh, rl) = left, right
    return mul(lh, rl, dims) + mul(ll, rh, dims) + mul(lh, rh, dims)


def times(left, right):
    return close(parts(left), parts(right))


def far(*arrays):
    return [pltpu.with_memory_space_constraint(a, pltpu.HBM) for a in arrays]


def prepare_kernel(lot, uol, ldn, udn, lin, uin, lio, uio, *out):
    x_new, y_new, upper_pair, upper_triple, lower_pair, lower_triple, side_high, side_low = out
    width = lin.shape[0]
    upper = times(uol[...].T, uio[...].T)
    lower = times(lio[...].T, lot[...].T)
    x_new[...] = times(ldn[...].T, lin[...].T)
    y_new[...] = times(uin[...].T, udn[...].T)
    upper_pair[...] = upper
    lower_pair[...] = lower
    triple = times(uin[...].T, upper)
    upper_triple[...] = triple
    side_high[:width, :], side_low[:width, :] = parts(triple)
    side_high[width:, :], side_low[width:, :] = parts(-uio[...].T)
    lower_triple[...] = times(lower, lin[...].T)


def prepare(*factors):
    width = factors[0].shape[0]
    return pl.pallas_call(
        prepare_kernel,
        out_shape=(jax.ShapeDtypeStruct((width, width), FULL),) * 6
        + (jax.ShapeDtypeStruct((2 * width, width), HALF),) * 2,
        in_specs=[VMEM] * len(factors),
        out_specs=(VMEM,) * 8,
        name="prepare",
        cost_estimate=pl.CostEstimate(
            flops=36 * width**3, bytes_accessed=56 * width**2, transcendentals=0
        ),
    )(*factors)


def lower_rows(lower, panel, count, piece):
    return jnp.concatenate(
        [
            lower[pl.ds((2 * k + panel) * piece, piece), :]
            for k in range(count)
        ],
        axis=0,
    )


def band_kernel(count, triple, lio, lower, trail, out, weights):
    width = lio.shape[0]
    piece = width // count

    @pl.when(pl.program_id(0) == 0)
    def _():
        new = parts(lower_rows(lower, 0, count, piece))
        old = parts(lower_rows(lower, 1, count, piece))
        weight = close(parts(triple[...]), new) - close(parts(lio[...].T), old)
        weights[:width, :], weights[width:, :] = parts(weight)

    high, low = parts(trail[...])
    both = mul(weights[...], high, ((1,), (0,)))
    band = mul(weights[:width, :], low, ((1,), (0,))) + both[width:, :] + both[:width, :]
    size = out.shape[1]
    for k in range(out.shape[0]):
        out[k] = band[k * size : (k + 1) * size, :]


def band_products(triple, lio, lower, trail, ranks, count, tile=1024):
    rows, columns = trail.shape
    width = lio.shape[0]
    once = pl.Buffered(1)
    triple, lio, lower, trail = far(triple, lio, lower, trail)
    return pl.pallas_call(
        functools.partial(band_kernel, count),
        out_shape=jax.ShapeDtypeStruct((ranks, width // ranks, columns), FULL),
        grid=(columns // tile,),
        in_specs=[
            pl.BlockSpec((width, width), lambda j: (0, 0), pipeline_mode=once),
            pl.BlockSpec((width, width), lambda j: (0, 0), pipeline_mode=once),
            pl.BlockSpec((2 * width, rows), lambda j: (0, 0), pipeline_mode=once),
            pl.BlockSpec((rows, tile), lambda j: (0, j)),
        ],
        out_specs=pl.BlockSpec((ranks, width // ranks, tile), lambda j: (0, 0, j)),
        scratch_shapes=[pltpu.VMEM((2 * width, rows), HALF)],
        compiler_params=pltpu.CompilerParams(vmem_limit_bytes=24 << 20),
        name="band_products",
        cost_estimate=pl.CostEstimate(
            flops=6 * width * rows * columns,
            bytes_accessed=4 * (rows * columns + 2 * width * rows + width * columns),
            transcendentals=0,
        ),
    )(triple, lio, lower, trail)


def panel_kernel(count, tile, place, side_high, side_low, lower, trail, *rest):
    pieces = rest[:8]
    mine, other, strip, upper_high, upper_low, inner = rest[8:]
    width = side_high.shape[1]
    z, y, x, c = place[0], place[1], place[2], place[3]
    piece = width // count

    def assemble():
        inner[...] = jnp.zeros_like(inner)
        chunk = pieces[0].shape[0] // 4
        for k in range(8):
            for q in range(4):
                rank = 4 * (z ^ (k - 4)) + q if k >= 4 else 4 * q + (y ^ k)
                start = (k // 4) * width + rank * chunk
                at = pl.ds(pl.multiple_of(start, chunk), chunk)
                upper_high[at, :], upper_low[at, :] = parts(
                    pieces[k][q * chunk : (q + 1) * chunk, :]
                )

    def step(lower_tile, trail_tile, strip_tile):
        pl.when(pl.program_id(0) == 0)(assemble)
        product = close(
            parts(trail_tile[...]), (upper_high[...], upper_low[...]), ((1,), (1,))
        )
        product = parts(product)
        strip_tile[...] = close(product, (side_high[...], side_low[...]))
        for panel in range(2):
            left = parts(lower_rows(lower_tile, panel, count, piece))
            inner[panel * width : (panel + 1) * width, :] += close(left, product)

    pltpu.emit_pipeline(
        step,
        grid=(trail.shape[0] // tile,),
        in_specs=[
            pl.BlockSpec((lower.shape[0], tile), lambda i: (0, i)),
            pl.BlockSpec((tile, trail.shape[1]), lambda i: (i, 0)),
        ],
        out_specs=[pl.BlockSpec((tile, width), lambda i: (i, 0))],
    )(lower, trail, strip)

    rows, share = mine.shape[2], width // 4
    for k in range(4):
        for p in range(mine.shape[1]):
            start, column = (x ^ k) * share + rows * (p // 2), width * (p % 2)
            near = pl.ds(pl.multiple_of(c * width + start, rows), rows)
            beside = pl.ds(pl.multiple_of((1 - c) * width + start, rows), rows)
            mine[k, p] = inner[near, column : column + width]
            other[k, p] = inner[beside, column : column + width]


def panel_products(place, sides, lower, trail, pieces, count, tile=256):
    rows, columns = trail.shape
    width = sides[0].shape[1]
    share = (4, 16, width // 32, width)
    *sides, lower, trail = far(*sides, lower, trail)
    hbm = pl.BlockSpec(memory_space=pltpu.HBM)
    return pl.pallas_call(
        functools.partial(panel_kernel, count, tile),
        out_shape=(
            jax.ShapeDtypeStruct(share, FULL),
            jax.ShapeDtypeStruct(share, FULL),
            jax.ShapeDtypeStruct((rows, width), FULL),
        ),
        in_specs=[pl.BlockSpec(memory_space=pltpu.SMEM)] + [VMEM] * 2 + [hbm] * 2 + [VMEM] * 8,
        out_specs=(VMEM, VMEM, hbm),
        scratch_shapes=[pltpu.VMEM((2 * width, columns), HALF)] * 2
        + [pltpu.VMEM((2 * width, 2 * width), FULL)],
        compiler_params=pltpu.CompilerParams(vmem_limit_bytes=36 << 20),
        name="panel_products",
        cost_estimate=pl.CostEstimate(
            flops=3 * (4 * width * rows * columns + 12 * width * width * rows),
            bytes_accessed=4 * (rows * columns + 2 * width * columns + 4 * width * rows),
            transcendentals=0,
        ),
    )(place, *sides, lower, trail, *pieces)


def finish_kernel(
    place,
    mine,
    other,
    x_new,
    y_new,
    upper_pair,
    upper_triple,
    lower_pair,
    lower_triple,
    lot,
    uol,
    lin,
    uin,
    ldo,
    udo,
    lio,
    uio,
    corner_out,
    top_out,
    left_out,
    inner,
):
    width = lin.shape[0]
    c = place[3]
    rows, share = mine.shape[1], width // 4
    for k in range(4):
        for p in range(mine.shape[0] // 4):
            start, column = k * share + rows * (p // 2), width * (p % 2)
            near = pl.ds(pl.multiple_of(c * width + start, rows), rows)
            beside = pl.ds(pl.multiple_of((1 - c) * width + start, rows), rows)
            inner[near, column : column + width] = mine[4 * p + k]
            inner[beside, column : column + width] = other[4 * p + k]
    row = lax.broadcasted_iota(jnp.int32, (width, width), 0)
    column = lax.broadcasted_iota(jnp.int32, (width, width), 1)
    below = row > column
    g11, g12 = inner[:width, :width], inner[:width, width:]
    g21, g22 = inner[width:, :width], inner[width:, width:]
    lin_t, uin_t, lio_t, uio_t = lin[...].T, uin[...].T, lio[...].T, uio[...].T
    inside = jnp.where(below, times(x_new[...], g11), times(g11, y_new[...]))
    corner = times(times(lin_t, inside), uin_t)
    top = times(times(lin_t, g12), uio_t) - times(corner, upper_pair[...])
    left = times(lio_t, times(g21, uin_t)) - times(lower_pair[...], corner)
    top_out[...] = top
    left_out[...] = left
    outer = times(lower_triple[...], g12) - times(lio_t, g22)
    under = times(g21, upper_triple[...]) - times(g22, uio_t)
    lower_grad = -(times(left, uol[...].T) + outer)
    upper_grad = -(times(lot[...].T, top) + under)
    inside = jnp.where(
        below, times(ldo[...].T, lower_grad), times(upper_grad, udo[...].T)
    )
    corner_out[...] = times(times(lio_t, inside), uio_t)


def finish(place, mine, other, *factors):
    width = factors[0].shape[0]
    mine, other = (pltpu.with_memory_space_constraint(a, pltpu.VMEM) for a in (mine, other))
    return pl.pallas_call(
        finish_kernel,
        out_shape=(jax.ShapeDtypeStruct((width, width), FULL),) * 3,
        in_specs=[pl.BlockSpec(memory_space=pltpu.SMEM)] + [VMEM] * (2 + len(factors)),
        out_specs=(VMEM,) * 3,
        scratch_shapes=[pltpu.VMEM((2 * width, 2 * width), FULL)],
        name="finish",
        cost_estimate=pl.CostEstimate(
            flops=240 * width**3, bytes_accessed=84 * width**2, transcendentals=0
        ),
    )(place, mine, other, *factors)


def swap(value, axis, step):
    size = lax.axis_size(axis)
    return lax.ppermute(value, axis, [(i, i ^ step) for i in range(size)])


def exchange(value, axes):
    return lax.all_to_all(value, axes, 0, 0, tiled=True)


def pieces_of(value, axis):
    return [value] + [swap(value, axis, step) for step in range(1, lax.axis_size(axis))]


def placed(pieces, axis):
    me = lax.axis_index(axis)
    size = pieces[0].shape[0]
    out = jnp.zeros((len(pieces) * size, *pieces[0].shape[1:]), pieces[0].dtype)
    for step, piece in enumerate(pieces):
        out = lax.dynamic_update_slice_in_dim(out, piece, (me ^ step) * size, 0)
    return out


def together(*values):
    return lax.optimization_barrier(values)


def body(
    trail,
    lower_new,
    upper_new,
    lot,
    lower_old,
    uol,
    upper_old,
    ldn,
    udn,
    lin,
    uin,
    ldo,
    udo,
    lio,
    uio,
):
    row, col = ("z", "y"), ("x", "c")
    count = lax.axis_size(col)
    ranks = lax.axis_size(row)

    lower_mine = jnp.concatenate((lower_new.T, lower_old.T), axis=0)
    lower_stack = lax.all_gather(lower_mine, col, axis=0, tiled=True)
    small = prepare(lot, uol, ldn, udn, lin, uin, lio, uio)
    *near, small = together(*pieces_of(upper_new, "z"), *pieces_of(upper_old, "y"), small)
    near_new, near_old = together(placed(near[:4], "z"), placed(near[4:], "y"))
    pieces = pieces_of(near_new, "y") + pieces_of(near_old, "z")
    *small, side_high, side_low = small

    band = band_products(small[5], lio, lower_stack, trail, ranks, count)
    *pieces, _ = together(*pieces, band)
    band = lax.all_to_all(band, row, 0, 0, tiled=True)

    place = jnp.stack([lax.axis_index(a) for a in row + col]).astype(jnp.int32)
    mine, other, strip = panel_products(
        place, (side_high, side_low), lower_stack, trail, pieces, count
    )
    mine = mine + swap(other, "c", 1)
    mine = mine[0] + sum(swap(mine[k], "x", k) for k in (1, 2, 3))
    mine, band = together(mine, band.sum(0))
    band_right = -lax.all_gather(-band, row, axis=0, tiled=True)
    mine = exchange(mine, row).sum(0)
    mine = exchange(jnp.broadcast_to(mine[None], (4 * ranks, *mine.shape)), row + ("x",))
    mine, strip = together(mine, strip)
    strip = exchange(strip.reshape(count, -1, strip.shape[1]), col)
    other = swap(mine, "c", 1)
    corner_old, strip_top, band_left = finish(
        place, mine, other, *small, lot, uol, lin, uin, ldo, udo, lio, uio
    )
    strip, corner_old, band_right = together(strip, corner_old, band_right)
    return corner_old, strip_top, strip.sum(0), band_left, band_right


def solution(mesh):
    fine = Mesh(mesh.devices.reshape(4, 4, 4, 2), ("z", "y", "x", "c"))
    row, col = ("z", "y"), ("x", "c")
    split, whole = P(row, col), P()
    return jax.shard_map(
        body,
        mesh=fine,
        in_specs=(split, split, split, whole, split, whole, split) + (whole,) * 8,
        out_specs=(whole, whole, P(row + col, None), whole, P(None, col)),
        check_vma=False,
    )
```
